32 devices in a mesh: crop: 2 (over x), row: 8 (over z, y), col: 2 (over core).
Axes of the slice: x: 2, y: 2, z: 4, core: 2. Of those that a mesh axis runs over, the one named last changes fastest.
Arguments:
- pair_rep: bfloat16 [96, 48, 128], P(('crop', 'row'), 'col'), parts along dimension 0, may hold values from -6 to 6
- cotangent: bfloat16 [96, 48, 128], P(('crop', 'row'), 'col'), parts along dimension 0, may hold values from -6 to 6
- norm_gain: float32 [128], replicated, may hold values from 0.5 to 1.5
- norm_bias: float32 [128], replicated, may hold values from -3 to 3
- proj_weight: bfloat16 [128, 512], replicated, may hold values from -0.5 to 0.5
- gate_weight: bfloat16 [128, 128], replicated, may hold values from -0.5 to 0.5
- tri_gain: float32 [128], replicated, may hold values from 0.5 to 1.5
- tri_bias: float32 [128], replicated, may hold values from -3 to 3
- out_weight: bfloat16 [128, 128], replicated, may hold values from -0.5 to 0.5
Outputs:
- block_out: bfloat16 [96, 48, 128], P(('crop', 'row'), 'col'), parts along dimension 0
- pair_grad: float32 [96, 48, 128], P(('crop', 'row'), 'col'), parts along dimension 0
- proj_grad: float32 [256, 512], P('crop'), parts along dimension 0
- gate_grad: float32 [256, 128], P('crop'), parts along dimension 0
- out_grad: float32 [256, 128], P('crop'), parts along dimension 0
The draws below stay inside these ranges and needn't reach their ends.
There are 2 independent parts, one for each index of `crop`. The reference program is written for one: setup_inputs(seed, part) draws one part's arguments, and reference() takes and returns one part's arrays. A program takes and returns all parts, laid end to end along the dimension named above; an argument that names none is the same for every part. Nothing has to cross between parts.
All inputs are finite; a program needn't handle non-finite values.
Results may differ from the reference program's by a relative error of at most 0.0066.
Values may be sent and summed in bfloat16 or wider, within the bound.
A program may use at most 128 MiB of HBM per device.

```python
import jax
import jax.numpy as jnp
from jax import lax

C = 128
H = 128
N = 48


def block_scale(key, dims, cuts, smallest, top_value):
    def one(position, parts):
        heights = jax.random.uniform(jax.random.fold_in(jax.random.fold_in(key, 6), position), (parts,), jnp.float32, smallest / len(cuts), top_value / len(cuts))
        return jnp.repeat(jnp.exp(heights), dims[position] // parts).reshape((-1,) + (1,) * (len(dims) - position - 1))

    level = one(*cuts[0])
    for cut in cuts[1:]:
        level = level * one(*cut)
    return level


def noise(stream_key, shape, spread, most, shards=(), held_as=jnp.bfloat16):
    loudness = block_scale(stream_key, shape, shards, -0.22, 0.18) if shards else 1.0
    array = jax.random.normal(stream_key, shape, jnp.float32) * spread * loudness
    return jnp.minimum(jnp.maximum(array, -most), most).astype(held_as)


def setup_inputs(seed: int = 0, part: int = 0) -> dict:
    key_list = jax.random.split(jax.random.key(seed), 10)
    part_keys = jax.random.split(jax.random.fold_in(key_list[9], part), 10)
    pair_rep = noise(part_keys[0], (N, N, C), 1.0, 6.0, ((0, 8), (1, 2)))
    cotangent = noise(part_keys[1], (N, N, C), 1.0, 6.0, ((0, 8), (1, 2)))
    norm_gain = jnp.clip(1.0 + 0.1 * jax.random.normal(key_list[2], (C,), jnp.float32), 0.5, 1.5)
    norm_bias = noise(key_list[3], (C,), 0.5, 3.0, (), jnp.float32)
    proj_weight = noise(key_list[4], (C, 4 * H), C ** -0.5, 0.5)
    gate_weight = noise(key_list[5], (C, C), C ** -0.5, 0.5)
    tri_gain = jnp.clip(1.0 + 0.1 * jax.random.normal(key_list[6], (H,), jnp.float32), 0.5, 1.5)
    tri_bias = noise(key_list[7], (H,), 0.5, 3.0, (), jnp.float32)
    out_weight = noise(key_list[8], (H, C), H ** -0.5, 0.5)
    return dict(pair_rep=pair_rep, cotangent=cotangent, norm_gain=norm_gain, norm_bias=norm_bias, proj_weight=proj_weight, gate_weight=gate_weight, tri_gain=tri_gain, tri_bias=tri_bias, out_weight=out_weight)


def layer_norm(values, gain, bias):
    centred = values - lax.optimization_barrier(jnp.mean(values, axis=-1, keepdims=True))
    inverse = lax.rsqrt(lax.optimization_barrier(jnp.mean(centred * centred, axis=-1, keepdims=True)) + 1e-05)
    scaled = centred * inverse
    return (scaled * gain + bias, scaled, inverse)

def norm_back(grads, gain, scaled, inverse):
    weighted = grads * gain
    first = lax.optimization_barrier(jnp.mean(weighted, axis=-1, keepdims=True))
    second = lax.optimization_barrier(jnp.mean(weighted * scaled, axis=-1, keepdims=True))
    return inverse * (weighted - first - scaled * second)

def reference(pair_rep, cotangent, norm_gain, norm_bias, proj_weight, gate_weight, tri_gain, tri_bias, out_weight):
    f32 = jnp.float32
    bf16 = jnp.bfloat16
    normed_f, pair_hat, pair_inv = layer_norm(pair_rep.astype(f32), norm_gain, norm_bias)
    normed = normed_f.astype(bf16)
    flat_norm = normed.reshape(N * N, C)
    projected = jnp.dot(flat_norm, proj_weight, preferred_element_type=f32).reshape(N, N, 4 * H)
    sig_left = jax.nn.sigmoid(projected[..., 0:H])
    val_left = projected[..., H:2 * H]
    sig_right = jax.nn.sigmoid(projected[..., 2 * H:3 * H])
    val_right = projected[..., 3 * H:4 * H]
    left_edge = (sig_left * val_left).astype(bf16)
    right_edge = (sig_right * val_right).astype(bf16)
    out_gate = jax.nn.sigmoid(jnp.dot(flat_norm, gate_weight, preferred_element_type=f32).reshape(N, N, C))
    triangle = jnp.einsum('ikc,jkc->ijc', left_edge.astype(f32), right_edge.astype(f32))
    tri_f, tri_hat, tri_inv = layer_norm(triangle, tri_gain, tri_bias)
    tri_norm = tri_f.astype(bf16)
    flat_tri = tri_norm.reshape(N * N, H)
    update = jnp.dot(flat_tri, out_weight, preferred_element_type=f32).reshape(N, N, C)
    block_out = (out_gate * update).astype(bf16)
    cot = cotangent.astype(f32)
    d_update = (cot * out_gate).astype(bf16)
    d_gate = (cot * update * out_gate * (1.0 - out_gate)).astype(bf16)
    d_norm = jnp.dot(d_update.reshape(N * N, C), out_weight.T, preferred_element_type=f32).reshape(N, N, H)
    d_triangle = norm_back(d_norm, tri_gain, tri_hat, tri_inv).astype(bf16)
    d_left = jnp.einsum('ijc,jkc->ikc', d_triangle.astype(f32), right_edge.astype(f32))
    d_right = jnp.einsum('ijc,ikc->jkc', d_triangle.astype(f32), left_edge.astype(f32))
    d_proj = jnp.concatenate([d_left * val_left * sig_left * (1.0 - sig_left), d_left * sig_left, d_right * val_right * sig_right * (1.0 - sig_right), d_right * sig_right], axis=-1).astype(bf16)
    flat_dproj = d_proj.reshape(N * N, 4 * H)
    flat_dgate = d_gate.reshape(N * N, C)
    d_normed = jnp.dot(flat_dproj, proj_weight.T, preferred_element_type=f32) + jnp.dot(flat_dgate, gate_weight.T, preferred_element_type=f32)
    pair_grad = norm_back(d_normed.reshape(N, N, C), norm_gain, pair_hat, pair_inv)
    proj_grad = jnp.dot(flat_norm.T, flat_dproj, preferred_element_type=f32) / N
    gate_grad = jnp.dot(flat_norm.T, flat_dgate, preferred_element_type=f32) / N
    out_grad = jnp.dot(flat_tri.T, d_update.reshape(N * N, C), preferred_element_type=f32) / N
    return (block_out, pair_grad, proj_grad, gate_grad, out_grad)
```

```python
import functools

import jax
import jax.numpy as jnp
from jax import lax
from jax.experimental import pallas as pl
from jax.experimental.pallas import tpu as pltpu
from jax.sharding import PartitionSpec as P

F32 = jnp.float32
BF16 = jnp.bfloat16


def mean_last(values):
    return jnp.mean(values, axis=-1, keepdims=True)


def normalise(values):
    centred = values - mean_last(values)
    inverse = lax.rsqrt(mean_last(centred * centred) + 1e-05)
    return centred * inverse, inverse


def norm_back(weighted, scaled, inverse):
    return inverse * (weighted - mean_last(weighted) - scaled * mean_last(weighted * scaled))


def dot(a, b, ca=1, cb=0):
    return lax.dot_general(a, b, (((ca,), (cb,)), ((), ())), preferred_element_type=F32)


def kernel(
    R, Q, rows, K, H, C,
    x_hbm, cot_hbm, ng_hbm, nb_hbm, pw_hbm, gw_hbm, tg_hbm, tb_hbm, ow_hbm,
    out_ref, pg_ref, gall_ref,
    x_ref, cot_ref, ng_ref, nb_ref, pw_ref, gw_ref, tg_ref, tb_ref, ow_ref,
    gath, right32, left32, coef, og_s, hat_s, inv_s, dupd_s, dn,
    tri_s, tri_rcv, d32, dsend, drecv, dcol32,
    gsend, grecv, gfin,
    in_s, gath_ss, gath_rs, tri_ss, tri_rs, dn_ss, dn_rs, dcol_ss, dcol_rs,
    gs_ss, gs_rs, gf_ss, gf_rs,
):
    r = lax.axis_index("row")
    q = lax.axis_index("col")
    M = rows * K
    N = rows * R
    NP = R * Q
    RPQ = R // Q
    pad = -(-rows // 8) * 8
    me = r * Q + q

    def remote(src, dst, ss, rs, rr, qq):
        return pltpu.make_async_remote_copy(
            src_ref=src, dst_ref=dst, send_sem=ss, recv_sem=rs,
            device_id={"row": rr, "col": qq}, device_id_type=pl.DeviceIdType.MESH,
        )

    def loop(lo, hi, body):
        if hi - lo <= 16:
            for t in range(lo, hi):
                body(t)
            return

        def step(t, carry):
            body(t)
            return carry
        lax.fori_loop(lo, hi, step, 0)

    def wrap(value, size):
        return jnp.where(value >= size, value - size, value)

    def peer(t):
        rr, qq = wrap(r + t // Q, R), wrap(q + t % Q, Q)
        return rr, qq, rr * Q + qq

    def mate(t):
        if R & (R - 1):
            return lax.rem(r + t, R)
        out, bit = 0, 1
        while bit < R:
            out = out + bit * ((r // bit + t // bit) % 2)
            bit *= 2
        return out

    def back(t):
        return lax.rem(r + R - t, R) if R & (R - 1) else mate(t)

    barrier = pltpu.get_barrier_semaphore()

    def greet(t):
        rr, qq, _ = peer(t)
        pl.semaphore_signal(
            barrier, inc=1,
            device_id={"row": rr, "col": qq},
            device_id_type=pl.DeviceIdType.MESH,
        )

    loop(1, NP, greet)

    fetch = [
        pltpu.make_async_copy(src, dst, in_s.at[n]) for n, (src, dst) in enumerate((
            (x_hbm, x_ref), (ng_hbm, ng_ref), (nb_hbm, nb_ref), (pw_hbm, pw_ref),
            (gw_hbm, gw_ref), (cot_hbm, cot_ref), (ow_hbm, ow_ref), (tg_hbm, tg_ref),
            (tb_hbm, tb_ref),
        ))
    ]
    for copy in fetch:
        copy.start()

    piece = 2 * C // NP
    per = NP // 2

    def scatter(g, t):
        rr, qq, other = peer(t)
        return remote(
            gsend.at[g, other], grecv.at[g, me], gs_ss.at[g], gs_rs.at[g], rr, qq
        )

    def scatter_all(g):
        block = pl.ds(0, NP - 1)
        return remote(
            gsend.at[g, block], grecv.at[g, block], gs_ss.at[g], gs_rs.at[g], r, q
        )

    def scatter_start(g, first, second):
        for p in range(per):
            gsend[g, p] = first[p * piece : (p + 1) * piece, :].astype(BF16)
            gsend[g, per + p] = second[p * piece : (p + 1) * piece, :].astype(BF16)
        loop(1, NP, lambda t: scatter(g, t).start())
        grecv[g, me] = gsend[g, me]

    def spread(g, t):
        rr, qq, _ = peer(t)
        return remote(gfin.at[g, me], gfin.at[g, me], gf_ss.at[g], gf_rs.at[g], rr, qq)

    def spread_all(g):
        block = pl.ds(0, NP - 1)
        return remote(gfin.at[g, block], gfin.at[g, block], gf_ss.at[g], gf_rs.at[g], r, q)

    def spread_start(g):
        scatter_all(g).wait_recv()
        total = grecv[g, 0].astype(F32)
        for p in range(1, NP):
            total = total + grecv[g, p].astype(F32)
        gfin[g, me] = (total / N).astype(BF16)
        loop(1, NP, lambda t: spread(g, t).start())

    def gather(t):
        return remote(
            gath.at[r], gath.at[r], gath_ss.at[t], gath_rs.at[r], mate(t), q
        )

    def gather_from(t):
        source = back(t)
        return source, remote(
            gath.at[r], gath.at[source], gath_ss.at[t], gath_rs.at[source], source, q
        )

    def edge(gate, value):
        sig = jax.nn.sigmoid(gate)
        return (sig * value).astype(BF16).astype(F32), sig

    for n in range(3):
        fetch[n].wait()
    hat, inv = normalise(x_ref[...].astype(F32))
    normed = (hat * ng_ref[...] + nb_ref[...]).astype(BF16)
    hat_s[...] = hat
    inv_s[...] = jnp.broadcast_to(inv, hat.shape)
    gath[r] = normed

    own = pl.multiple_of(r * M, 8)
    fetch[3].wait()
    proj = dot(normed, pw_ref[...])
    vl, vr = proj[:, H : 2 * H], proj[:, 3 * H :]
    left_edge, sl = edge(proj[:, :H], vl)
    right_edge, sr = edge(proj[:, 2 * H : 3 * H], vr)
    left32[pl.ds(own, M), :] = left_edge
    right32[pl.ds(own, M), :] = right_edge
    coef[0] = vl * sl * (1.0 - sl)
    coef[1] = sl
    coef[2] = vr * sr * (1.0 - sr)
    coef[3] = sr
    for n in range(4, 9):
        fetch[n].wait()
    og = jax.nn.sigmoid(dot(normed, gw_ref[...]))
    og_s[...] = og
    d_update = (cot_ref[...].astype(F32) * og).astype(BF16)
    dupd_s[...] = d_update
    dn_own = dot(d_update, ow_ref[...], 1, 1) * tg_ref[...]
    dn[q] = dn_own
    for b in range(RPQ):
        parts = []
        for i in range(rows):
            block = dn_own[i * K + b * rows : i * K + (b + 1) * rows, :]
            if pad > rows:
                block = jnp.concatenate([block, jnp.zeros((pad - rows, H), F32)], axis=0)
            parts.append(block)
        dsend[b] = jnp.concatenate(parts, axis=0).astype(BF16)
    mine = r // RPQ == q

    @pl.when(mine)
    def _():
        drecv[r] = dsend[lax.rem(r, RPQ)]

    pl.semaphore_wait(barrier, NP - 1)

    loop(0, R - 1, lambda t: gather(R - 1 - t).start())

    def dn_copy(t, slot, other):
        return remote(dn.at[q], dn.at[slot], dn_ss.at[t], dn_rs.at[slot], r, other)

    for t in range(1, Q):
        dn_copy(t, q, wrap(q + t, Q)).start()

    def each_target(act):
        for t in range(Q):
            def one(b, t=t):
                target = q * RPQ + b
                other = wrap(q + t, Q)
                if t:
                    act(b, t, target, other)
                else:
                    @pl.when(target != r)
                    def _():
                        act(b, t, target, other)
            loop(0, RPQ, one)

    def col_copy(b, t, target, other):
        return remote(
            dsend.at[b], drecv.at[r], dcol_ss.at[t * RPQ + b], dcol_rs.at[r], target, other
        )

    each_target(lambda b, t, target, other: col_copy(b, t, target, other).start())

    def arrive(t):
        source, copy = gather_from(t)
        copy.wait_recv()
        proj = dot(gath[source], pw_ref[...])
        place = pl.ds(pl.multiple_of(source * M, 8), M)
        left32[place, :] = edge(proj[:, :H], proj[:, H : 2 * H])[0]
        right32[place, :] = edge(proj[:, 2 * H : 3 * H], proj[:, 3 * H :])[0]
    loop(1, R, arrive)

    def zeros():
        return tuple(jnp.zeros((K, H), F32) for _ in range(rows))

    def partial(part, half):
        ours, theirs = (left32, right32) if part == 0 else (right32, left32)
        base = half * (K * K)

        def step(k, accs):
            block = theirs[pl.ds(base + k, K, stride=K), :]
            return tuple(
                accs[i] + ours[pl.ds(own + i * K + k, 1), :] * block for i in range(rows)
            )
        accs = lax.fori_loop(0, K, step, zeros(), unroll=4)
        for i in range(rows):
            tri_s[part, half, i * K : (i + 1) * K, :] = accs[i]

    def tri_copy(part, half, t, slot, other):
        return remote(
            tri_s.at[part, half], tri_rcv.at[slot, part, half],
            tri_ss.at[part, half, t], tri_rs.at[slot, part, half], r, other,
        )

    order = [(0, wrap(q + t, Q)) for t in range(1, Q)] + [(0, q)] + [(1, h) for h in range(Q)]
    for part, half in order:
        partial(part, half)
        for t in range(1, Q):
            tri_copy(part, half, t, q, wrap(q + t, Q)).start()

    owner = r // RPQ

    def col_wait(t):
        source = wrap(r + R - t, R)
        remote(
            dsend.at[0], drecv.at[source], dcol_ss.at[0], dcol_rs.at[source], source, owner
        ).wait_recv()
    loop(1, R, col_wait)

    @pl.when(jnp.logical_not(mine))
    def _():
        remote(dsend.at[0], drecv.at[r], dcol_ss.at[0], dcol_rs.at[r], r, owner).wait_recv()

    def widen_col(t):
        dcol32[pl.ds(pl.multiple_of(t * rows * pad, 8), rows * pad), :] = drecv[t].astype(F32)
    loop(0, R, widen_col)

    for t in range(1, Q):
        other = wrap(q + t, Q)
        dn_copy(t, other, other).wait_recv()

    def complete(part, half):
        triangle = tri_s[part, half]
        for t in range(1, Q):
            other = wrap(q + t, Q)
            tri_copy(part, half, t, other, other).wait_recv()
            triangle = triangle + tri_rcv[other, part, half]
        if part == 0:
            weighted = dn[half]
        else:
            weighted = jnp.concatenate(
                [dcol32[pl.ds(half * K * pad + j, K, stride=pad), :] for j in range(rows)], axis=0
            )
        tri_hat, tri_inv = normalise(triangle)
        d_tri = norm_back(weighted, tri_hat, tri_inv).astype(BF16)
        d32[part, pl.ds(pl.multiple_of(half * M, 8), M), :] = d_tri.astype(F32)
        return tri_hat

    tri_hat = complete(0, q)
    tri_norm = (tri_hat * tg_ref[...] + tb_ref[...]).astype(BF16)
    update = dot(tri_norm, ow_ref[...])
    og = og_s[...]
    out_ref[...] = (og * update).astype(BF16)
    d_gate = (cot_ref[...].astype(F32) * update * og * (1.0 - og)).astype(BF16)
    normed = gath[r]
    scatter_start(0, dot(normed, d_gate, 0, 0), dot(tri_norm, dupd_s[...], 0, 0))
    for t in range(1, Q):
        complete(0, wrap(q + t, Q))

    def pull(part):
        theirs = right32 if part == 0 else left32
        accs = zeros()
        for h in range(Q):
            def step(j, accs, h=h):
                block = theirs[pl.ds(pl.multiple_of((h * K + j) * K, 8), K), :]
                return tuple(
                    accs[i] + d32[part, pl.ds(h * M + i * K + j, 1), :] * block
                    for i in range(rows)
                )
            accs = lax.fori_loop(0, K, step, accs, unroll=4)
        grad = jnp.concatenate(accs, axis=0)
        first = (grad * coef[2 * part]).astype(BF16)
        second = (grad * coef[2 * part + 1]).astype(BF16)
        wide = dot(normed, jnp.concatenate([first, second], axis=-1), 0, 0)
        scatter_start(1 + part, wide[:, :H], wide[:, H:])
        return [first, second]

    d_proj = pull(0)
    for h in range(Q):
        complete(1, h)
    d_proj += pull(1)

    d_cat = jnp.concatenate(d_proj, axis=-1)
    d_normed = dot(d_cat, pw_ref[...], 1, 1) + dot(d_gate, gw_ref[...], 1, 1)
    pg_ref[...] = norm_back(d_normed * ng_ref[...], hat_s[...], inv_s[...])

    for g in range(3):
        spread_start(g)

    loop(1, R, lambda t: gather(t).wait_send())
    for t in range(1, Q):
        other = wrap(q + t, Q)
        dn_copy(t, q, other).wait_send()
        for part in range(2):
            for half in range(Q):
                tri_copy(part, half, t, q, other).wait_send()
    each_target(lambda b, t, target, other: col_copy(b, t, target, other).wait_send())
    for g in range(3):
        scatter_all(g).wait_send()
        spread_all(g).wait_recv()
    gall_ref[...] = gfin[...]
    for g in range(3):
        spread_all(g).wait_send()


def finish(NP, piece, C, H, block_ref, grad_ref, gall_ref, out_ref, pg_ref, gp_ref, gg_ref, go_ref):
    out_ref[...] = block_ref[...]
    pg_ref[...] = grad_ref[...]
    targets = (
        (gg_ref, 0), (go_ref, 0), (gp_ref, 0), (gp_ref, H), (gp_ref, 2 * H), (gp_ref, 3 * H),
    )
    per = C // piece
    for t, (ref, col) in enumerate(targets):
        for p in range(per):
            whole = (t % 2) * per + p
            ref[p * piece : (p + 1) * piece, col : col + H] = gall_ref[t // 2, whole].astype(F32)


def local(R, Q, pair_rep, cotangent, ng, nb, pw, gw, tg, tb, ow):
    rows, K, C = pair_rep.shape
    H = tg.shape[0]
    M = rows * K
    NP = R * Q
    RPQ = R // Q
    pad = -(-rows // 8) * 8
    piece = 2 * C // NP
    dma = pltpu.SemaphoreType.DMA
    vmem = pltpu.VMEM
    spec = pl.BlockSpec(memory_space=pltpu.VMEM)
    shapes = (
        jax.ShapeDtypeStruct((M, C), BF16),
        jax.ShapeDtypeStruct((M, C), F32),
        jax.ShapeDtypeStruct((3, NP, piece, H), BF16),
    )
    any_spec = pl.BlockSpec(memory_space=pl.ANY)
    parts = pl.pallas_call(
        functools.partial(kernel, R, Q, rows, K, H, C),
        out_shape=shapes,
        in_specs=[any_spec] * 9,
        out_specs=[spec] * 3,
        scratch_shapes=[
            vmem((M, C), BF16), vmem((M, C), BF16), vmem((1, C), F32), vmem((1, C), F32),
            vmem((C, 4 * H), BF16), vmem((C, C), BF16), vmem((1, H), F32), vmem((1, H), F32),
            vmem((H, C), BF16),
            vmem((R, M, C), BF16),
            vmem((R * M, H), F32),
            vmem((R * M, H), F32),
            vmem((4, M, H), F32),
            vmem((M, C), F32),
            vmem((M, C), F32),
            vmem((M, C), F32),
            vmem((M, C), BF16),
            vmem((Q, M, H), F32),
            vmem((2, Q, M, H), F32),
            vmem((Q, 2, Q, M, H), F32),
            vmem((2, Q * M, H), F32),
            vmem((RPQ, rows * pad, H), BF16),
            vmem((R, rows * pad, H), BF16),
            vmem((R * rows * pad, H), F32),
            vmem((3, NP, piece, H), BF16),
            vmem((3, NP, piece, H), BF16),
            vmem((3, NP, piece, H), BF16),
            dma((9,)),
            dma((R,)), dma((R,)),
            dma((2, Q, Q)), dma((Q, 2, Q)),
            dma((Q,)), dma((Q,)),
            dma((R,)), dma((R,)),
            dma((3,)), dma((3,)),
            dma((3,)), dma((3,)),
        ],
        compiler_params=pltpu.CompilerParams(
            collective_id=0, has_side_effects=True, vmem_limit_bytes=60 * 1024 * 1024
        ),
        name="triangle_step",
    )(
        pair_rep.reshape(M, C), cotangent.reshape(M, C), ng.reshape(1, C), nb.reshape(1, C),
        pw, gw, tg.reshape(1, H), tb.reshape(1, H), ow,
    )
    outs = pl.pallas_call(
        functools.partial(finish, NP, piece, C, H),
        out_shape=(
            shapes[0],
            shapes[1],
            jax.ShapeDtypeStruct((C, 4 * H), F32),
            jax.ShapeDtypeStruct((C, C), F32),
            jax.ShapeDtypeStruct((H, C), F32),
        ),
        in_specs=[spec] * 3,
        out_specs=[spec] * 5,
        name="finish",
    )(*parts)
    return (
        outs[0].reshape(rows, K, C), outs[1].reshape(rows, K, C), outs[2], outs[3], outs[4],
    )


def solution(mesh):
    tile = P(("crop", "row"), "col", None)
    grad = P("crop", None)
    return jax.shard_map(
        functools.partial(local, mesh.shape["row"], mesh.shape["col"]),
        mesh=mesh,
        in_specs=(tile, tile, P(), P(), P(), P(), P(), P(), P()),
        out_specs=(tile, tile, grad, grad, grad),
        check_vma=False,
    )
```

```python
import functools

import jax
import jax.numpy as jnp
from jax import lax
from jax.experimental import pallas as pl
from jax.experimental.pallas import tpu as pltpu
from jax.sharding import PartitionSpec as P

F32 = jnp.float32
BF16 = jnp.bfloat16


def mean_last(values):
    return jnp.mean(values, axis=-1, keepdims=True)


def normalise(values):
    centred = values - mean_last(values)
    inverse = lax.rsqrt(mean_last(centred * centred) + 1e-05)
    return centred * inverse, inverse


def norm_back(weighted, scaled, inverse):
    return inverse * (weighted - mean_last(weighted) - scaled * mean_last(weighted * scaled))


def dot(a, b, ca=1, cb=0):
    return lax.dot_general(a, b, (((ca,), (cb,)), ((), ())), preferred_element_type=F32)


def kernel(
    R, Q, rows, K, H, C,
    x_hbm, cot_hbm, ng_hbm, nb_hbm, pw_hbm, gw_hbm, tg_hbm, tb_hbm, ow_hbm,
    out_ref, pg_ref, gall_ref,
    x_ref, cot_ref, ng_ref, nb_ref, pw_ref, gw_ref, tg_ref, tb_ref, ow_ref,
    gath, right32, left32, coef, og_s, hat_s, inv_s, dupd_s, dn,
    tri_s, tri_rcv, d32, dsend, drecv, dcol32,
    gsend, grecv, gfin,
    in_s, gath_ss, gath_rs, tri_ss, tri_rs, dn_ss, dn_rs, dcol_ss, dcol_rs,
    gs_ss, gs_rs, gf_ss, gf_rs,
):
    r = lax.axis_index("row")
    q = lax.axis_index("col")
    M = rows * K
    N = rows * R
    NP = R * Q
    RPQ = R // Q
    pad = -(-rows // 8) * 8
    me = r * Q + q

    def remote(src, dst, ss, rs, rr, qq):
        return pltpu.make_async_remote_copy(
            src_ref=src, dst_ref=dst, send_sem=ss, recv_sem=rs,
            device_id={"row": rr, "col": qq}, device_id_type=pl.DeviceIdType.MESH,
        )

    def loop(lo, hi, body):
        if hi - lo <= 16:
            for t in range(lo, hi):
                body(t)
            return

        def step(t, carry):
            body(t)
            return carry
        lax.fori_loop(lo, hi, step, 0)

    def wrap(value, size):
        return jnp.where(value >= size, value - size, value)

    def peer(t):
        rr, qq = wrap(r + t // Q, R), wrap(q + t % Q, Q)
        return rr, qq, rr * Q + qq

    def mate(t):
        if R & (R - 1):
            return lax.rem(r + t, R)
        out, bit = 0, 1
        while bit < R:
            out = out + bit * ((r // bit + t // bit) % 2)
            bit *= 2
        return out

    def back(t):
        return lax.rem(r + R - t, R) if R & (R - 1) else mate(t)

    barrier = pltpu.get_barrier_semaphore()

    def greet(t):
        rr, qq, _ = peer(t)
        pl.semaphore_signal(
            barrier, inc=1,
            device_id={"row": rr, "col": qq},
            device_id_type=pl.DeviceIdType.MESH,
        )

    loop(1, NP, greet)

    fetch = [
        pltpu.make_async_copy(src, dst, in_s.at[n]) for n, (src, dst) in enumerate((
            (x_hbm, x_ref), (ng_hbm, ng_ref), (nb_hbm, nb_ref), (pw_hbm, pw_ref),
            (gw_hbm, gw_ref), (cot_hbm, cot_ref), (ow_hbm, ow_ref), (tg_hbm, tg_ref),
            (tb_hbm, tb_ref),
        ))
    ]
    for copy in fetch:
        copy.start()

    piece = 2 * C // NP
    per = NP // 2

    def scatter(g, t):
        rr, qq, other = peer(t)
        return remote(
            gsend.at[g, other], grecv.at[g, me], gs_ss.at[g], gs_rs.at[g], rr, qq
        )

    def scatter_all(g):
        block = pl.ds(0, NP - 1)
        return remote(
            gsend.at[g, block], grecv.at[g, block], gs_ss.at[g], gs_rs.at[g], r, q
        )

    def scatter_start(g, first, second):
        for p in range(per):
            gsend[g, p] = first[p * piece : (p + 1) * piece, :].astype(BF16)
            gsend[g, per + p] = second[p * piece : (p + 1) * piece, :].astype(BF16)
        loop(1, NP, lambda t: scatter(g, t).start())
        grecv[g, me] = gsend[g, me]

    def spread(g, t):
        rr, qq, _ = peer(t)
        return remote(gfin.at[g, me], gfin.at[g, me], gf_ss.at[g], gf_rs.at[g], rr, qq)

    def spread_all(g):
        block = pl.ds(0, NP - 1)
        return remote(gfin.at[g, block], gfin.at[g, block], gf_ss.at[g], gf_rs.at[g], r, q)

    def spread_start(g):
        scatter_all(g).wait_recv()
        total = grecv[g, 0].astype(F32)
        for p in range(1, NP):
            total = total + grecv[g, p].astype(F32)
        gfin[g, me] = (total / N).astype(BF16)
        loop(1, NP, lambda t: spread(g, t).start())

    def gather(t):
        return remote(
            gath.at[r], gath.at[r], gath_ss.at[t], gath_rs.at[r], mate(t), q
        )

    def gather_from(t):
        source = back(t)
        return source, remote(
            gath.at[r], gath.at[source], gath_ss.at[t], gath_rs.at[source], source, q
        )

    def edge(gate, value):
        sig = jax.nn.sigmoid(gate)
        return (sig * value).astype(BF16).astype(F32), sig

    for n in range(3):
        fetch[n].wait()
    hat, inv = normalise(x_ref[...].astype(F32))
    normed = (hat * ng_ref[...] + nb_ref[...]).astype(BF16)
    hat_s[...] = hat
    inv_s[...] = jnp.broadcast_to(inv, hat.shape)
    gath[r] = normed

    own = pl.multiple_of(r * M, 8)
    fetch[3].wait()
    proj = dot(normed, pw_ref[...])
    vl, vr = proj[:, H : 2 * H], proj[:, 3 * H :]
    left_edge, sl = edge(proj[:, :H], vl)
    right_edge, sr = edge(proj[:, 2 * H : 3 * H], vr)
    left32[pl.ds(own, M), :] = left_edge
    right32[pl.ds(own, M), :] = right_edge
    coef[0] = vl * sl * (1.0 - sl)
    coef[1] = sl
    coef[2] = vr * sr * (1.0 - sr)
    coef[3] = sr
    for n in range(4, 9):
        fetch[n].wait()
    og = jax.nn.sigmoid(dot(normed, gw_ref[...]))
    og_s[...] = og
    d_update = (cot_ref[...].astype(F32) * og).astype(BF16)
    dupd_s[...] = d_update
    dn_own = dot(d_update, ow_ref[...], 1, 1) * tg_ref[...]
    dn[q] = dn_own
    for b in range(RPQ):
        parts = []
        for i in range(rows):
            block = dn_own[i * K + b * rows : i * K + (b + 1) * rows, :]
            if pad > rows:
                block = jnp.concatenate([block, jnp.zeros((pad - rows, H), F32)], axis=0)
            parts.append(block)
        dsend[b] = jnp.concatenate(parts, axis=0).astype(BF16)
    mine = r // RPQ == q

    @pl.when(mine)
    def _():
        drecv[r] = dsend[lax.rem(r, RPQ)]

    pl.semaphore_wait(barrier, NP - 1)

    loop(0, R - 1, lambda t: gather(t + 1).start())

    def dn_copy(t, slot, other):
        return remote(dn.at[q], dn.at[slot], dn_ss.at[t], dn_rs.at[slot], r, other)

    for t in range(1, Q):
        dn_copy(t, q, wrap(q + t, Q)).start()

    def each_target(act):
        for t in range(Q):
            def one(b, t=t):
                target = q * RPQ + b
                other = wrap(q + t, Q)
                if t:
                    act(b, t, target, other)
                else:
                    @pl.when(target != r)
                    def _():
                        act(b, t, target, other)
            loop(0, RPQ, one)

    def col_copy(b, t, target, other):
        return remote(
            dsend.at[b], drecv.at[r], dcol_ss.at[t * RPQ + b], dcol_rs.at[r], target, other
        )

    each_target(lambda b, t, target, other: col_copy(b, t, target, other).start())

    def arrive(t):
        source, copy = gather_from(t)
        copy.wait_recv()
        proj = dot(gath[source], pw_ref[...])
        place = pl.ds(pl.multiple_of(source * M, 8), M)
        left32[place, :] = edge(proj[:, :H], proj[:, H : 2 * H])[0]
        right32[place, :] = edge(proj[:, 2 * H : 3 * H], proj[:, 3 * H :])[0]
    loop(1, R, arrive)

    def zeros():
        return tuple(jnp.zeros((K, H), F32) for _ in range(rows))

    def partial(part, half):
        ours, theirs = (left32, right32) if part == 0 else (right32, left32)
        base = half * (K * K)

        def step(k, accs):
            block = theirs[pl.ds(base + k, K, stride=K), :]
            return tuple(
                accs[i] + ours[pl.ds(own + i * K + k, 1), :] * block for i in range(rows)
            )
        accs = lax.fori_loop(0, K, step, zeros(), unroll=4)
        for i in range(rows):
            tri_s[part, half, i * K : (i + 1) * K, :] = accs[i]

    def tri_copy(part, half, t, slot, other):
        return remote(
            tri_s.at[part, half], tri_rcv.at[slot, part, half],
            tri_ss.at[part, half, t], tri_rs.at[slot, part, half], r, other,
        )

    order = [(0, wrap(q + t, Q)) for t in range(1, Q)] + [(0, q)] + [(1, h) for h in range(Q)]
    for part, half in order:
        partial(part, half)
        for t in range(1, Q):
            tri_copy(part, half, t, q, wrap(q + t, Q)).start()

    owner = r // RPQ

    def col_wait(t):
        source = wrap(r + R - t, R)
        remote(
            dsend.at[0], drecv.at[source], dcol_ss.at[0], dcol_rs.at[source], source, owner
        ).wait_recv()
    loop(1, R, col_wait)

    @pl.when(jnp.logical_not(mine))
    def _():
        remote(dsend.at[0], drecv.at[r], dcol_ss.at[0], dcol_rs.at[r], r, owner).wait_recv()

    def widen_col(t):
        dcol32[pl.ds(pl.multiple_of(t * rows * pad, 8), rows * pad), :] = drecv[t].astype(F32)
    loop(0, R, widen_col)

    for t in range(1, Q):
        other = wrap(q + t, Q)
        dn_copy(t, other, other).wait_recv()

    def complete(part, half):
        triangle = tri_s[part, half]
        for t in range(1, Q):
            other = wrap(q + t, Q)
            tri_copy(part, half, t, other, other).wait_recv()
            triangle = triangle + tri_rcv[other, part, half]
        if part == 0:
            weighted = dn[half]
        else:
            weighted = jnp.concatenate(
                [dcol32[pl.ds(half * K * pad + j, K, stride=pad), :] for j in range(rows)], axis=0
            )
        tri_hat, tri_inv = normalise(triangle)
        d_tri = norm_back(weighted, tri_hat, tri_inv).astype(BF16)
        d32[part, pl.ds(pl.multiple_of(half * M, 8), M), :] = d_tri.astype(F32)
        return tri_hat

    tri_hat = complete(0, q)
    tri_norm = (tri_hat * tg_ref[...] + tb_ref[...]).astype(BF16)
    update = dot(tri_norm, ow_ref[...])
    og = og_s[...]
    out_ref[...] = (og * update).astype(BF16)
    d_gate = (cot_ref[...].astype(F32) * update * og * (1.0 - og)).astype(BF16)
    normed = gath[r]
    scatter_start(0, dot(normed, d_gate, 0, 0), dot(tri_norm, dupd_s[...], 0, 0))
    for t in range(1, Q):
        complete(0, wrap(q + t, Q))

    def pull(part):
        theirs = right32 if part == 0 else left32
        accs = zeros()
        for h in range(Q):
            def step(j, accs, h=h):
                block = theirs[pl.ds(pl.multiple_of((h * K + j) * K, 8), K), :]
                return tuple(
                    accs[i] + d32[part, pl.ds(h * M + i * K + j, 1), :] * block
                    for i in range(rows)
                )
            accs = lax.fori_loop(0, K, step, accs, unroll=4)
        grad = jnp.concatenate(accs, axis=0)
        first = (grad * coef[2 * part]).astype(BF16)
        second = (grad * coef[2 * part + 1]).astype(BF16)
        wide = dot(normed, jnp.concatenate([first, second], axis=-1), 0, 0)
        scatter_start(1 + part, wide[:, :H], wide[:, H:])
        return [first, second]

    d_proj = pull(0)
    for h in range(Q):
        complete(1, h)
    d_proj += pull(1)

    d_cat = jnp.concatenate(d_proj, axis=-1)
    d_normed = dot(d_cat, pw_ref[...], 1, 1) + dot(d_gate, gw_ref[...], 1, 1)
    pg_ref[...] = norm_back(d_normed * ng_ref[...], hat_s[...], inv_s[...])

    for g in range(3):
        spread_start(g)

    loop(1, R, lambda t: gather(t).wait_send())
    for t in range(1, Q):
        other = wrap(q + t, Q)
        dn_copy(t, q, other).wait_send()
        for part in range(2):
            for half in range(Q):
                tri_copy(part, half, t, q, other).wait_send()
    each_target(lambda b, t, target, other: col_copy(b, t, target, other).wait_send())
    for g in range(3):
        scatter_all(g).wait_send()
        spread_all(g).wait_recv()
    gall_ref[...] = gfin[...]
    for g in range(3):
        spread_all(g).wait_send()


def finish(NP, piece, C, H, block_ref, grad_ref, gall_ref, out_ref, pg_ref, gp_ref, gg_ref, go_ref):
    out_ref[...] = block_ref[...]
    pg_ref[...] = grad_ref[...]
    targets = (
        (gg_ref, 0), (go_ref, 0), (gp_ref, 0), (gp_ref, H), (gp_ref, 2 * H), (gp_ref, 3 * H),
    )
    per = C // piece
    for t, (ref, col) in enumerate(targets):
        for p in range(per):
            whole = (t % 2) * per + p
            ref[p * piece : (p + 1) * piece, col : col + H] = gall_ref[t // 2, whole].astype(F32)


def local(R, Q, pair_rep, cotangent, ng, nb, pw, gw, tg, tb, ow):
    rows, K, C = pair_rep.shape
    H = tg.shape[0]
    M = rows * K
    NP = R * Q
    RPQ = R // Q
    pad = -(-rows // 8) * 8
    piece = 2 * C // NP
    dma = pltpu.SemaphoreType.DMA
    vmem = pltpu.VMEM
    spec = pl.BlockSpec(memory_space=pltpu.VMEM)
    shapes = (
        jax.ShapeDtypeStruct((M, C), BF16),
        jax.ShapeDtypeStruct((M, C), F32),
        jax.ShapeDtypeStruct((3, NP, piece, H), BF16),
    )
    any_spec = pl.BlockSpec(memory_space=pl.ANY)
    parts = pl.pallas_call(
        functools.partial(kernel, R, Q, rows, K, H, C),
        out_shape=tuple(pltpu.VMEM(v.shape, v.dtype) for v in shapes),
        in_specs=[any_spec] * 9,
        out_specs=[spec] * 3,
        scratch_shapes=[
            vmem((M, C), BF16), vmem((M, C), BF16), vmem((1, C), F32), vmem((1, C), F32),
            vmem((C, 4 * H), BF16), vmem((C, C), BF16), vmem((1, H), F32), vmem((1, H), F32),
            vmem((H, C), BF16),
            vmem((R, M, C), BF16),
            vmem((R * M, H), F32),
            vmem((R * M, H), F32),
            vmem((4, M, H), F32),
            vmem((M, C), F32),
            vmem((M, C), F32),
            vmem((M, C), F32),
            vmem((M, C), BF16),
            vmem((Q, M, H), F32),
            vmem((2, Q, M, H), F32),
            vmem((Q, 2, Q, M, H), F32),
            vmem((2, Q * M, H), F32),
            vmem((RPQ, rows * pad, H), BF16),
            vmem((R, rows * pad, H), BF16),
            vmem((R * rows * pad, H), F32),
            vmem((3, NP, piece, H), BF16),
            vmem((3, NP, piece, H), BF16),
            vmem((3, NP, piece, H), BF16),
            dma((9,)),
            dma((R,)), dma((R,)),
            dma((2, Q, Q)), dma((Q, 2, Q)),
            dma((Q,)), dma((Q,)),
            dma((R,)), dma((R,)),
            dma((3,)), dma((3,)),
            dma((3,)), dma((3,)),
        ],
        compiler_params=pltpu.CompilerParams(
            collective_id=0, has_side_effects=True, vmem_limit_bytes=60 * 1024 * 1024
        ),
        name="triangle_step",
    )(
        pair_rep.reshape(M, C), cotangent.reshape(M, C), ng.reshape(1, C), nb.reshape(1, C),
        pw, gw, tg.reshape(1, H), tb.reshape(1, H), ow,
    )
    outs = pl.pallas_call(
        functools.partial(finish, NP, piece, C, H),
        out_shape=(
            shapes[0],
            shapes[1],
            jax.ShapeDtypeStruct((C, 4 * H), F32),
            jax.ShapeDtypeStruct((C, C), F32),
            jax.ShapeDtypeStruct((H, C), F32),
        ),
        in_specs=[spec] * 3,
        out_specs=[spec] * 5,
        compiler_params=pltpu.CompilerParams(vmem_limit_bytes=4 * 1024 * 1024),
        name="finish",
    )(*parts)
    return (
        outs[0].reshape(rows, K, C), outs[1].reshape(rows, K, C), outs[2], outs[3], outs[4],
    )


def solution(mesh):
    tile = P(("crop", "row"), "col", None)
    grad = P("crop", None)
    return jax.shard_map(
        functools.partial(local, mesh.shape["row"], mesh.shape["col"]),
        mesh=mesh,
        in_specs=(tile, tile, P(), P(), P(), P(), P(), P(), P()),
        out_specs=(tile, tile, grad, grad, grad),
        check_vma=False,
    )
```

```python
import functools

import jax
import jax.numpy as jnp
from jax import lax
from jax.experimental import pallas as pl
from jax.experimental.pallas import tpu as pltpu
from jax.sharding import PartitionSpec as P

F32 = jnp.float32
BF16 = jnp.bfloat16


def mean_last(values):
    return jnp.mean(values, axis=-1, keepdims=True)


def normalise(values):
    centred = values - mean_last(values)
    inverse = lax.rsqrt(mean_last(centred * centred) + 1e-05)
    return centred * inverse, inverse


def norm_back(weighted, scaled, inverse):
    return inverse * (weighted - mean_last(weighted) - scaled * mean_last(weighted * scaled))


def dot(a, b, ca=1, cb=0):
    return lax.dot_general(a, b, (((ca,), (cb,)), ((), ())), preferred_element_type=F32)


def kernel(
    R, Q, rows, K, H, C,
    x_hbm, cot_hbm, ng_hbm, nb_hbm, pw_hbm, gw_hbm, tg_hbm, tb_hbm, ow_hbm,
    out_ref, pg_ref, gall_ref,
    x_ref, cot_ref, ng_ref, nb_ref, pw_ref, gw_ref, tg_ref, tb_ref, ow_ref,
    gath, right32, left32, coef, og_s, hat_s, inv_s, dupd_s, dn,
    hat2_s, tri_s, tri_rcv, d32, dsend, drecv, dcol32,
    csend, crecv, gkeep, gsend, grecv, gfin,
    in_s, gath_ss, gath_rs, tri_ss, tri_rs, dn_ss, dn_rs, dcol_ss, dcol_rs,
    near, hand_ss, hand_rs, cs_ss, cs_rs, gs_ss, gs_rs, gf_ss, gf_rs, sh_ss, sh_rs,
):
    r = lax.axis_index("row")
    q = lax.axis_index("col")
    M = rows * K
    N = rows * R
    NP = R * Q
    RPQ = R // Q
    pad = -(-rows // 8) * 8
    me = q * R + r
    direct_in, direct_out = (False, False, False), (False, False, True)
    mine_pieces = pl.ds(q * R, R)

    def remote(src, dst, ss, rs, rr, qq):
        return pltpu.make_async_remote_copy(
            src_ref=src, dst_ref=dst, send_sem=ss, recv_sem=rs,
            device_id={"row": rr, "col": qq}, device_id_type=pl.DeviceIdType.MESH,
        )

    def loop(lo, hi, body):
        if hi - lo <= 16:
            for t in range(lo, hi):
                body(t)
            return

        def step(t, carry):
            body(t)
            return carry
        lax.fori_loop(lo, hi, step, 0)

    def wrap(value, size):
        return jnp.where(value >= size, value - size, value)

    def peer(t):
        rr, qq = wrap(r + t // Q, R), wrap(q + t % Q, Q)
        return rr, qq, rr * Q + qq

    B = 2 if R % 2 == 0 else 1

    def mate(t):
        if R & (R - 1):
            return lax.rem(r + t, R)
        out, bit = 0, 1
        while bit < R:
            out = out + bit * ((r // bit + t // bit) % 2)
            bit *= 2
        return out

    def back(t):
        return lax.rem(r + R - t, R) if R & (R - 1) else mate(t)

    barrier = pltpu.get_barrier_semaphore()

    A = R // B

    def signal(sem, rr, qq):
        pl.semaphore_signal(
            sem, inc=1, device_id={"row": rr, "col": qq}, device_id_type=pl.DeviceIdType.MESH
        )

    loop(1, A, lambda t: signal(barrier, mate(t * B), q))
    for t in range(1, B):
        signal(barrier, mate(t), q)
    for t in range(1, Q):
        signal(barrier, r, wrap(q + t, Q))

    fetch = [
        pltpu.make_async_copy(src, dst, in_s.at[n]) for n, (src, dst) in enumerate((
            (x_hbm, x_ref), (ng_hbm, ng_ref), (nb_hbm, nb_ref), (pw_hbm, pw_ref),
            (gw_hbm, gw_ref), (cot_hbm, cot_ref), (ow_hbm, ow_ref), (tg_hbm, tg_ref),
            (tb_hbm, tb_ref),
        ))
    ]
    for copy in fetch:
        copy.start()

    piece = 2 * C // NP
    per = NP // 2

    def core_copy(g, t, slot, other):
        return remote(
            csend.at[g, t], crecv.at[g, slot], cs_ss.at[g, t], cs_rs.at[g, slot], r, other
        )

    def core_start(g, first, second):
        both = (first, second)

        def part(qq, rr):
            whole = rr * Q + qq
            p = whole % per
            return both[whole // per][p * piece : (p + 1) * piece, :]
        if direct_in[g]:
            for rr in range(R):
                for qq in range(Q):
                    gsend[g, qq * R + rr] = part(qq, rr).astype(BF16)
            scatter_go(g)
            return
        for t in range(Q):
            other = wrap(q + t, Q)
            for rr in range(R):
                block = part(Q - 1, rr)
                for qq in range(Q - 1):
                    block = jnp.where(other == qq, part(qq, rr), block)
                if t:
                    csend[g, t, rr] = block.astype(BF16)
                else:
                    gkeep[g, rr] = block
            if t:
                core_copy(g, t, q, other).start()

    def targets(straight):
        return [(t, u) for t in range(R) for u in range(Q if straight else 1) if t or u]

    def scatter(g, t, u):
        rr, qq = (mate(t) if t else r), wrap(q + u, Q)
        return remote(
            gsend.at[g, qq * R + rr], grecv.at[g, me],
            gs_ss.at[g], gs_rs.at[g], rr, qq
        )

    def scatter_all(g):
        block = pl.ds(0, len(targets(direct_in[g])))
        return remote(
            gsend.at[g, block], grecv.at[g, block], gs_ss.at[g], gs_rs.at[g], r, q
        )

    def scatter_go(g):
        for t, u in targets(direct_in[g]):
            scatter(g, t, u).start()
        grecv[g, me] = gsend[g, me]

    def scatter_start(g):
        if direct_in[g]:
            return
        total = gkeep[g]
        for t in range(1, Q):
            other = wrap(q + t, Q)
            core_copy(g, t, other, other).wait_recv()
            total = total + crecv[g, other].astype(F32)
        gsend[g, mine_pieces] = total.astype(BF16)
        scatter_go(g)

    def spread(g, t, u):
        rr, qq = (mate(t) if t else r), wrap(q + u, Q)
        return remote(gfin.at[g, me], gfin.at[g, me], gf_ss.at[g], gf_rs.at[g], rr, qq)

    def spread_all(g):
        block = pl.ds(0, len(targets(direct_out[g])))
        return remote(gfin.at[g, block], gfin.at[g, block], gf_ss.at[g], gf_rs.at[g], r, q)

    def spread_start(g):
        scatter_all(g).wait_recv()
        if direct_in[g]:
            parts = [grecv[g, p] for p in range(NP)]
        else:
            kept = grecv[g, mine_pieces]
            parts = [kept[p] for p in range(R)]
        total = parts[0].astype(F32)
        for p in parts[1:]:
            total = total + p.astype(F32)
        gfin[g, me] = (total / N).astype(BF16)
        for t, u in targets(direct_out[g]):
            spread(g, t, u).start()

    def share(g, t, other, slot):
        block = pl.ds(slot * R, R)
        return remote(
            gfin.at[g, block], gfin.at[g, block], sh_ss.at[g, t], sh_rs.at[g, slot], r, other
        )

    def gather(t):
        return remote(
            gath.at[r], gath.at[r], gath_ss.at[t], gath_rs.at[r], mate(t), q
        )

    def gather_from(t):
        source = back(t)
        return source, remote(
            gath.at[r], gath.at[source], gath_ss.at[t], gath_rs.at[source], source, q
        )

    def edge(gate, value):
        sig = jax.nn.sigmoid(gate)
        return (sig * value).astype(BF16).astype(F32), sig

    for n in range(3):
        fetch[n].wait()
    hat, inv = normalise(x_ref[...].astype(F32))
    normed = (hat * ng_ref[...] + nb_ref[...]).astype(BF16)
    hat_s[...] = hat
    inv_s[...] = jnp.broadcast_to(inv, hat.shape)
    gath[r] = normed

    own = pl.multiple_of(r * M, 8)
    fetch[3].wait()
    proj = dot(normed, pw_ref[...])
    vl, vr = proj[:, H : 2 * H], proj[:, 3 * H :]
    left_edge, sl = edge(proj[:, :H], vl)
    right_edge, sr = edge(proj[:, 2 * H : 3 * H], vr)
    left32[pl.ds(own, M), :] = left_edge
    right32[pl.ds(own, M), :] = right_edge
    coef[0] = vl * sl * (1.0 - sl)
    coef[1] = sl
    coef[2] = vr * sr * (1.0 - sr)
    coef[3] = sr
    for n in range(4, 9):
        fetch[n].wait()
    og = jax.nn.sigmoid(dot(normed, gw_ref[...]))
    og_s[...] = og
    d_update = (cot_ref[...].astype(F32) * og).astype(BF16)
    dupd_s[...] = d_update
    dn_own = dot(d_update, ow_ref[...], 1, 1) * tg_ref[...]
    dn_own = dn_own - mean_last(dn_own)
    dn[q] = dn_own
    for b in range(RPQ):
        parts = []
        for i in range(rows):
            block = dn_own[i * K + b * rows : i * K + (b + 1) * rows, :]
            if pad > rows:
                block = jnp.concatenate([block, jnp.zeros((pad - rows, H), F32)], axis=0)
            parts.append(block)
        dsend[b] = jnp.concatenate(parts, axis=0).astype(BF16)
    mine = r // RPQ == q

    @pl.when(mine)
    def _():
        drecv[r] = dsend[lax.rem(r, RPQ)]

    pl.semaphore_wait(barrier, A + B + Q - 3)
    for t in range(1, B):
        signal(near, mate(t), q)
    for t in range(1, B):
        gather(t).start()
    loop(1, A, lambda t: gather(t * B).start())
    if B > 1:
        pl.semaphore_wait(near, B - 1)
        loop(1, A, lambda t: [gather(t * B + u).start() for u in range(1, B)])

    def dn_copy(t, slot, other):
        return remote(dn.at[q], dn.at[slot], dn_ss.at[t], dn_rs.at[slot], r, other)

    for t in range(1, Q):
        dn_copy(t, q, wrap(q + t, Q)).start()

    def each_target(act):
        def one(b):
            target = q * RPQ + b

            @pl.when(target != r)
            def _():
                act(b, target)
        loop(0, RPQ, one)

    def col_copy(b, target):
        return remote(dsend.at[b], drecv.at[r], dcol_ss.at[b], dcol_rs.at[r], target, q)

    each_target(lambda b, target: col_copy(b, target).start())

    def hand_on(t, other):
        return remote(drecv, drecv, hand_ss.at[t], hand_rs, r, other)

    def arrive(t):
        source, copy = gather_from(t)
        copy.wait_recv()
        proj = dot(gath[source], pw_ref[...])
        place = pl.ds(pl.multiple_of(source * M, 8), M)
        left32[place, :] = edge(proj[:, :H], proj[:, H : 2 * H])[0]
        right32[place, :] = edge(proj[:, 2 * H : 3 * H], proj[:, 3 * H :])[0]
    def zeros():
        return tuple(jnp.zeros((K, H), F32) for _ in range(rows))

    def partial(part, half):
        ours, theirs = (left32, right32) if part == 0 else (right32, left32)
        base = half * (K * K)

        def step(k, accs):
            block = theirs[pl.ds(base + k, K, stride=K), :]
            return tuple(
                accs[i] + ours[pl.ds(own + i * K + k, 1), :] * block for i in range(rows)
            )
        accs = lax.fori_loop(0, K, step, zeros(), unroll=4)
        for i in range(rows):
            tri_s[part, half, i * K : (i + 1) * K, :] = accs[i]

    def tri_copy(part, half, t, slot, other):
        return remote(
            tri_s.at[part, half], tri_rcv.at[slot, part, half],
            tri_ss.at[part, half, t], tri_rs.at[slot, part, half], r, other,
        )

    split = not R & (R - 1)
    halves = [mate(g * RPQ) // RPQ if split else g for g in range(Q)]
    if not split:
        loop(1, R, arrive)
    for g, half in enumerate(halves):
        if split:
            loop(max(1, g * RPQ), (g + 1) * RPQ, arrive)
        for part in range(2):
            partial(part, half)
            for t in range(1, Q):
                tri_copy(part, half, t, q, wrap(q + t, Q)).start()

    @pl.when(mine)
    def _():
        def col_wait(t):
            source = back(t)
            remote(
                dsend.at[0], drecv.at[source], dcol_ss.at[0], dcol_rs.at[source], source, q
            ).wait_recv()
        loop(1, R, col_wait)
        for t in range(1, Q):
            hand_on(t, wrap(q + t, Q)).start()

    for t in range(1, Q):
        other = wrap(q + t, Q)
        dn_copy(t, other, other).wait_recv()

    def complete(part, which):
        sums, weights = [], []
        for half in which:
            for t in range(1, Q):
                other = wrap(q + t, Q)
                tri_copy(part, half, t, other, other).wait_recv()
        for half in which:
            triangle = tri_s[part, half]
            for t in range(1, Q):
                triangle = triangle + tri_rcv[wrap(q + t, Q), part, half]
            sums.append(triangle)
            if part == 0:
                weights.append(dn[half])
            else:
                weights += [
                    dcol32[pl.ds(half * (K * pad) + j, K, stride=pad), :] for j in range(rows)
                ]
        weighted = jnp.concatenate(weights, axis=0)
        tri_hat, tri_inv = normalise(jnp.concatenate(sums, axis=0))
        d_tri = tri_inv * (weighted - tri_hat * mean_last(weighted * tri_hat))
        d_tri = d_tri.astype(BF16).astype(F32)
        for n, half in enumerate(which):
            d32[part, pl.ds(pl.multiple_of(half * M, 8), M), :] = d_tri[n * M : (n + 1) * M, :]
            if part == 0:
                hat2_s[half] = tri_hat[n * M : (n + 1) * M, :]

    def pull(part, which, accs):
        theirs = right32 if part == 0 else left32
        for half in which:
            def step(j, accs, half=half):
                block = theirs[pl.ds(pl.multiple_of((half * K + j) * K, 8), K), :]
                return tuple(
                    accs[i] + d32[part, pl.ds(half * M + i * K + j, 1), :] * block
                    for i in range(rows)
                )
            accs = lax.fori_loop(0, K, step, accs, unroll=4)
        return accs

    normed = gath[r]

    def settle(part, accs):
        grad = jnp.concatenate(accs, axis=0)
        first = (grad * coef[2 * part]).astype(BF16)
        second = (grad * coef[2 * part + 1]).astype(BF16)
        wide = dot(normed, jnp.concatenate([first, second], axis=-1), 0, 0)
        core_start(1 + part, wide[:, :H], wide[:, H:])
        return [first, second]

    def strips():
        @pl.when(jnp.logical_not(mine))
        def _():
            hand_on(0, r // RPQ).wait_recv()

        def widen_col(t):
            dcol32[pl.ds(pl.multiple_of(t * rows * pad, 8), rows * pad), :] = drecv[t].astype(F32)
        loop(0, R, widen_col)

    def gates():
        tri_norm = (hat2_s[q] * tg_ref[...] + tb_ref[...]).astype(BF16)
        update = dot(tri_norm, ow_ref[...])
        og = og_s[...]
        out_ref[...] = (og * update).astype(BF16)
        d_gate = (cot_ref[...].astype(F32) * update * og * (1.0 - og)).astype(BF16)
        core_start(0, dot(normed, d_gate, 0, 0), dot(tri_norm, dupd_s[...], 0, 0))
        return d_gate

    soon, late = halves[: Q - 1], halves[Q - 1 :]
    complete(0, soon)
    accs = pull(0, soon, zeros())
    complete(0, late)
    d_gate = gates()
    d_proj = settle(0, pull(0, late, accs))
    scatter_start(0)
    strips()
    complete(1, halves)
    d_proj += settle(1, pull(1, halves, zeros()))
    scatter_start(1)
    d_cat = jnp.concatenate(d_proj, axis=-1)
    d_normed = dot(d_cat, pw_ref[...], 1, 1) + dot(d_gate, gw_ref[...], 1, 1)
    pg_ref[...] = norm_back(d_normed * ng_ref[...], hat_s[...], inv_s[...])

    scatter_start(2)
    for g in range(3):
        spread_start(g)

    loop(1, R, lambda t: gather(t).wait_send())
    for t in range(1, Q):
        other = wrap(q + t, Q)
        dn_copy(t, q, other).wait_send()
        for part in range(2):
            for half in range(Q):
                tri_copy(part, half, t, q, other).wait_send()
    each_target(lambda b, target: col_copy(b, target).wait_send())

    @pl.when(mine)
    def _():
        for t in range(1, Q):
            hand_on(t, wrap(q + t, Q)).wait_send()

    for g in range(3):
        spread_all(g).wait_recv()
        if not direct_out[g]:
            for t in range(1, Q):
                share(g, t, wrap(q + t, Q), q).start()
    for g in range(3):
        scatter_all(g).wait_send()
        spread_all(g).wait_send()
        if not direct_in[g]:
            for t in range(1, Q):
                core_copy(g, t, q, wrap(q + t, Q)).wait_send()
    for g in range(3):
        if not direct_out[g]:
            for t in range(1, Q):
                other = wrap(q + t, Q)
                share(g, t, other, other).wait_recv()
    gall_ref[...] = gfin[...]
    for g in range(3):
        if not direct_out[g]:
            for t in range(1, Q):
                share(g, t, wrap(q + t, Q), q).wait_send()


def finish(Q, R, piece, C, H, block_ref, grad_ref, gall_ref, out_ref, pg_ref, gp_ref, gg_ref, go_ref):
    out_ref[...] = block_ref[...]
    pg_ref[...] = grad_ref[...]
    targets = (
        (gg_ref, 0), (go_ref, 0), (gp_ref, 0), (gp_ref, H), (gp_ref, 2 * H), (gp_ref, 3 * H),
    )
    per = C // piece
    for t, (ref, col) in enumerate(targets):
        for p in range(per):
            whole = (t % 2) * per + p
            ref[p * piece : (p + 1) * piece, col : col + H] = gall_ref[t // 2, whole % Q * R + whole // Q].astype(F32)


def local(R, Q, pair_rep, cotangent, ng, nb, pw, gw, tg, tb, ow):
    rows, K, C = pair_rep.shape
    H = tg.shape[0]
    M = rows * K
    NP = R * Q
    RPQ = R // Q
    pad = -(-rows // 8) * 8
    piece = 2 * C // NP
    dma = pltpu.SemaphoreType.DMA
    vmem = pltpu.VMEM
    spec = pl.BlockSpec(memory_space=pltpu.VMEM)
    shapes = (
        jax.ShapeDtypeStruct((M, C), BF16),
        jax.ShapeDtypeStruct((M, C), F32),
        jax.ShapeDtypeStruct((3, NP, piece, H), BF16),
    )
    any_spec = pl.BlockSpec(memory_space=pl.ANY)
    parts = pl.pallas_call(
        functools.partial(kernel, R, Q, rows, K, H, C),
        out_shape=tuple(pltpu.VMEM(v.shape, v.dtype) for v in shapes),
        in_specs=[any_spec] * 9,
        out_specs=[spec] * 3,
        scratch_shapes=[
            vmem((M, C), BF16), vmem((M, C), BF16), vmem((1, C), F32), vmem((1, C), F32),
            vmem((C, 4 * H), BF16), vmem((C, C), BF16), vmem((1, H), F32), vmem((1, H), F32),
            vmem((H, C), BF16),
            vmem((R, M, C), BF16),
            vmem((R * M, H), F32),
            vmem((R * M, H), F32),
            vmem((4, M, H), F32),
            vmem((M, C), F32),
            vmem((M, C), F32),
            vmem((M, C), F32),
            vmem((M, C), BF16),
            vmem((Q, M, H), F32),
            vmem((Q, M, H), F32),
            vmem((2, Q, M, H), F32),
            vmem((Q, 2, Q, M, H), F32),
            vmem((2, Q * M, H), F32),
            vmem((RPQ, rows * pad, H), BF16),
            vmem((R, rows * pad, H), BF16),
            vmem((R * rows * pad, H), F32),
            vmem((3, Q, R, piece, H), BF16),
            vmem((3, Q, R, piece, H), BF16),
            vmem((3, R, piece, H), F32),
            vmem((3, NP, piece, H), BF16),
            vmem((3, NP, piece, H), BF16),
            vmem((3, NP, piece, H), BF16),
            dma((9,)),
            dma((R,)), dma((R,)),
            dma((2, Q, Q)), dma((Q, 2, Q)),
            dma((Q,)), dma((Q,)),
            dma((R,)), dma((R,)),
            pltpu.SemaphoreType.REGULAR, dma((Q,)), dma,
            dma((3, Q)), dma((3, Q)),
            dma((3,)), dma((3,)),
            dma((3,)), dma((3,)),
            dma((3, Q)), dma((3, Q)),
        ],
        compiler_params=pltpu.CompilerParams(
            collective_id=0, has_side_effects=True, vmem_limit_bytes=60 * 1024 * 1024
        ),
        name="triangle_step",
    )(
        pair_rep.reshape(M, C), cotangent.reshape(M, C), ng.reshape(1, C), nb.reshape(1, C),
        pw, gw, tg.reshape(1, H), tb.reshape(1, H), ow,
    )
    outs = pl.pallas_call(
        functools.partial(finish, Q, R, piece, C, H),
        out_shape=(
            shapes[0],
            shapes[1],
            jax.ShapeDtypeStruct((C, 4 * H), F32),
            jax.ShapeDtypeStruct((C, C), F32),
            jax.ShapeDtypeStruct((H, C), F32),
        ),
        in_specs=[spec] * 3,
        out_specs=[spec] * 5,
        compiler_params=pltpu.CompilerParams(vmem_limit_bytes=4 * 1024 * 1024),
        name="finish",
    )(*parts)
    return (
        outs[0].reshape(rows, K, C), outs[1].reshape(rows, K, C), outs[2], outs[3], outs[4],
    )


def solution(mesh):
    tile = P(("crop", "row"), "col", None)
    grad = P("crop", None)
    return jax.shard_map(
        functools.partial(local, mesh.shape["row"], mesh.shape["col"]),
        mesh=mesh,
        in_specs=(tile, tile, P(), P(), P(), P(), P(), P(), P()),
        out_specs=(tile, tile, grad, grad, grad),
        check_vma=False,
    )
```

```python
import functools

import jax
import jax.numpy as jnp
from jax import lax
from jax.experimental import pallas as pl
from jax.experimental.pallas import tpu as pltpu
from jax.sharding import PartitionSpec as P

F32 = jnp.float32
BF16 = jnp.bfloat16


def mean_last(values):
    return jnp.mean(values, axis=-1, keepdims=True)


def normalise(values):
    centred = values - mean_last(values)
    inverse = lax.rsqrt(mean_last(centred * centred) + 1e-05)
    return centred * inverse, inverse


def norm_back(weighted, scaled, inverse):
    return inverse * (weighted - mean_last(weighted) - scaled * mean_last(weighted * scaled))


def dot(a, b, ca=1, cb=0):
    return lax.dot_general(a, b, (((ca,), (cb,)), ((), ())), preferred_element_type=F32)


def kernel(
    R, Q, rows, K, H, C,
    x_hbm, cot_hbm, ng_hbm, nb_hbm, pw_hbm, gw_hbm, tg_hbm, tb_hbm, ow_hbm,
    out_ref, pg_ref, gall_ref,
    x_ref, cot_ref, ng_ref, nb_ref, pw_ref, gw_ref, tg_ref, tb_ref, ow_ref,
    gath, right32, left32, coef, og_s, hat_s, inv_s, dupd_s, dn,
    hat2_s, tri_s, tri_rcv, d32, dsend, drecv, dcol32,
    csend, crecv, gkeep, gsend, grecv, gfin,
    in_s, gath_ss, gath_rs, tri_ss, tri_rs, dn_ss, dn_rs, dcol_ss, dcol_rs,
    near, hand_ss, hand_rs, cs_ss, cs_rs, gs_ss, gs_rs, gf_ss, gf_rs, sh_ss, sh_rs,
):
    r = lax.axis_index("row")
    q = lax.axis_index("col")
    M = rows * K
    N = rows * R
    NP = R * Q
    RPQ = R // Q
    pad = -(-rows // 8) * 8
    me = q * R + r
    direct_in, direct_out = (False, False, False), (False, True, True)
    mine_pieces = pl.ds(q * R, R)

    def remote(src, dst, ss, rs, rr, qq):
        return pltpu.make_async_remote_copy(
            src_ref=src, dst_ref=dst, send_sem=ss, recv_sem=rs,
            device_id={"row": rr, "col": qq}, device_id_type=pl.DeviceIdType.MESH,
        )

    def loop(lo, hi, body):
        if hi - lo <= 16:
            for t in range(lo, hi):
                body(t)
            return

        def step(t, carry):
            body(t)
            return carry
        lax.fori_loop(lo, hi, step, 0)

    def wrap(value, size):
        return jnp.where(value >= size, value - size, value)

    def peer(t):
        rr, qq = wrap(r + t // Q, R), wrap(q + t % Q, Q)
        return rr, qq, rr * Q + qq

    B = 2 if R > 1 and not R & (R - 1) else 1

    def mate(t):
        if R & (R - 1):
            return lax.rem(r + t, R)
        out, bit = 0, 1
        while bit < R:
            out = out + bit * ((r // bit + t // bit) % 2)
            bit *= 2
        return out

    def back(t):
        return lax.rem(r + R - t, R) if R & (R - 1) else mate(t)

    barrier = pltpu.get_barrier_semaphore()

    A = R // B

    def signal(sem, rr, qq):
        pl.semaphore_signal(
            sem, inc=1, device_id={"row": rr, "col": qq}, device_id_type=pl.DeviceIdType.MESH
        )

    loop(1, A, lambda t: signal(barrier, mate(t * B), q))
    for t in range(1, B):
        signal(barrier, mate(t), q)
    for t in range(1, Q):
        signal(barrier, r, wrap(q + t, Q))

    fetch = [
        pltpu.make_async_copy(src, dst, in_s.at[n]) for n, (src, dst) in enumerate((
            (x_hbm, x_ref), (ng_hbm, ng_ref), (nb_hbm, nb_ref), (pw_hbm, pw_ref),
            (gw_hbm, gw_ref), (cot_hbm, cot_ref), (ow_hbm, ow_ref), (tg_hbm, tg_ref),
            (tb_hbm, tb_ref),
        ))
    ]
    for copy in fetch:
        copy.start()

    piece = 2 * C // NP
    per = NP // 2

    def core_copy(g, t, slot, other):
        return remote(
            csend.at[g, t], crecv.at[g, slot], cs_ss.at[g, t], cs_rs.at[g, slot], r, other
        )

    def core_start(g, first, second):
        both = (first, second)

        def part(qq, rr):
            whole = rr * Q + qq
            p = whole % per
            return both[whole // per][p * piece : (p + 1) * piece, :]
        if direct_in[g]:
            for rr in range(R):
                for qq in range(Q):
                    gsend[g, qq * R + rr] = part(qq, rr).astype(BF16)
            scatter_go(g)
            return
        for t in range(Q):
            other = wrap(q + t, Q)
            for rr in range(R):
                block = part(Q - 1, rr)
                for qq in range(Q - 1):
                    block = jnp.where(other == qq, part(qq, rr), block)
                if t:
                    csend[g, t, rr] = block.astype(BF16)
                else:
                    gkeep[g, rr] = block
            if t:
                core_copy(g, t, q, other).start()

    def targets(straight):
        return [(t, u) for t in range(R) for u in range(Q if straight else 1) if t or u]

    def scatter(g, t, u):
        rr, qq = (mate(t) if t else r), wrap(q + u, Q)
        return remote(
            gsend.at[g, qq * R + rr], grecv.at[g, me],
            gs_ss.at[g], gs_rs.at[g], rr, qq
        )

    def scatter_all(g):
        block = pl.ds(0, len(targets(direct_in[g])))
        return remote(
            gsend.at[g, block], grecv.at[g, block], gs_ss.at[g], gs_rs.at[g], r, q
        )

    def scatter_go(g):
        for t, u in targets(direct_in[g]):
            scatter(g, t, u).start()
        grecv[g, me] = gsend[g, me]

    def scatter_start(g):
        if direct_in[g]:
            return
        total = gkeep[g]
        for t in range(1, Q):
            other = wrap(q + t, Q)
            core_copy(g, t, other, other).wait_recv()
            total = total + crecv[g, other].astype(F32)
        gsend[g, mine_pieces] = total.astype(BF16)
        scatter_go(g)

    def spread(g, t, u):
        rr, qq = (mate(t) if t else r), wrap(q + u, Q)
        return remote(gfin.at[g, me], gfin.at[g, me], gf_ss.at[g], gf_rs.at[g], rr, qq)

    def spread_all(g):
        block = pl.ds(0, len(targets(direct_out[g])))
        return remote(gfin.at[g, block], gfin.at[g, block], gf_ss.at[g], gf_rs.at[g], r, q)

    def spread_start(g):
        scatter_all(g).wait_recv()
        if direct_in[g]:
            parts = [grecv[g, p] for p in range(NP)]
        else:
            kept = grecv[g, mine_pieces]
            parts = [kept[p] for p in range(R)]
        total = parts[0].astype(F32)
        for p in parts[1:]:
            total = total + p.astype(F32)
        gfin[g, me] = (total / N).astype(BF16)
        for t, u in targets(direct_out[g]):
            spread(g, t, u).start()

    def share(g, t, other, slot):
        block = pl.ds(slot * R, R)
        return remote(
            gfin.at[g, block], gfin.at[g, block], sh_ss.at[g, t], sh_rs.at[g, slot], r, other
        )

    lead = M // 3 // 16 * 16 if B > 1 else 0
    head, rest, whole = pl.ds(0, lead), pl.ds(lead, M - lead), pl.ds(0, M)

    def block_copy(kind, src, t, lane, other):
        span = (head, rest, whole, head)[kind]
        return remote(
            gath.at[src, span], gath.at[src, span], gath_ss.at[kind, t], gath_rs.at[lane, src],
            other, q,
        )

    def line_head(t):
        return block_copy(0, r, t, 0, mate(t))

    def gather(t):
        return block_copy(2 if t_is_one(t) or not lead else 1, r, t, 1, mate(t))

    def t_is_one(t):
        return isinstance(t, int) and t == 1

    def relay(t):
        return block_copy(3, back(t), t, 0, mate(1))

    def head_wait(t):
        block_copy(0, back(t), t, 0, back(t)).wait_recv()

    def edge(gate, value):
        sig = jax.nn.sigmoid(gate)
        return (sig * value).astype(BF16).astype(F32), sig

    for n in range(3):
        fetch[n].wait()
    hat, inv = normalise(x_ref[...].astype(F32))
    normed = (hat * ng_ref[...] + nb_ref[...]).astype(BF16)
    hat_s[...] = hat
    inv_s[...] = jnp.broadcast_to(inv, hat.shape)
    gath[r] = normed

    own = pl.multiple_of(r * M, 8)
    fetch[3].wait()
    proj = dot(normed, pw_ref[...])
    vl, vr = proj[:, H : 2 * H], proj[:, 3 * H :]
    left_edge, sl = edge(proj[:, :H], vl)
    right_edge, sr = edge(proj[:, 2 * H : 3 * H], vr)
    left32[pl.ds(own, M), :] = left_edge
    right32[pl.ds(own, M), :] = right_edge
    coef[0] = vl * sl * (1.0 - sl)
    coef[1] = sl
    coef[2] = vr * sr * (1.0 - sr)
    coef[3] = sr
    for n in range(4, 9):
        fetch[n].wait()
    og = jax.nn.sigmoid(dot(normed, gw_ref[...]))
    og_s[...] = og
    d_update = (cot_ref[...].astype(F32) * og).astype(BF16)
    dupd_s[...] = d_update
    dn_own = dot(d_update, ow_ref[...], 1, 1) * tg_ref[...]
    dn_own = dn_own - mean_last(dn_own)
    dn[q] = dn_own
    for b in range(RPQ):
        parts = []
        for i in range(rows):
            block = dn_own[i * K + b * rows : i * K + (b + 1) * rows, :]
            if pad > rows:
                block = jnp.concatenate([block, jnp.zeros((pad - rows, H), F32)], axis=0)
            parts.append(block)
        dsend[b] = jnp.concatenate(parts, axis=0).astype(BF16)
    mine = r // RPQ == q

    @pl.when(mine)
    def _():
        drecv[r] = dsend[lax.rem(r, RPQ)]

    pl.semaphore_wait(barrier, A + B + Q - 3)
    for t in range(1, B):
        signal(near, mate(t), q)
    if B > 1:
        if lead:
            loop(1, A, lambda t: line_head(t * B).start())
        gather(1).start()
        pl.semaphore_wait(near, B - 1)
        loop(1, A, lambda t: [gather(t * B + u).start() for u in range(B)])
    else:
        loop(1, R, lambda t: gather(t).start())

    def dn_copy(t, slot, other):
        return remote(dn.at[q], dn.at[slot], dn_ss.at[t], dn_rs.at[slot], r, other)

    for t in range(1, Q):
        dn_copy(t, q, wrap(q + t, Q)).start()

    def each_target(act):
        def one(b):
            target = q * RPQ + b

            @pl.when(target != r)
            def _():
                act(b, target)
        loop(0, RPQ, one)

    def col_copy(b, target):
        return remote(dsend.at[b], drecv.at[r], dcol_ss.at[b], dcol_rs.at[r], target, q)

    each_target(lambda b, target: col_copy(b, target).start())

    def hand_on(t, other):
        return remote(drecv, drecv, hand_ss.at[t], hand_rs, r, other)

    def arrive(t, odd):
        source = back(t)
        block_copy(2 if t_is_one(t) or not lead else 1, source, t, 1, source).wait_recv()
        if lead and odd:
            block_copy(0, source, t, 0, mate(1)).wait_recv()
        proj = dot(gath[source], pw_ref[...])
        place = pl.ds(pl.multiple_of(source * M, 8), M)
        left32[place, :] = edge(proj[:, :H], proj[:, H : 2 * H])[0]
        right32[place, :] = edge(proj[:, 2 * H : 3 * H], proj[:, 3 * H :])[0]
    def zeros():
        return tuple(jnp.zeros((K, H), F32) for _ in range(rows))

    def partial(part, half):
        ours, theirs = (left32, right32) if part == 0 else (right32, left32)
        base = half * (K * K)

        def step(k, accs):
            block = theirs[pl.ds(base + k, K, stride=K), :]
            return tuple(
                accs[i] + ours[pl.ds(own + i * K + k, 1), :] * block for i in range(rows)
            )
        accs = lax.fori_loop(0, K, step, zeros(), unroll=8)
        for i in range(rows):
            tri_s[part, half, i * K : (i + 1) * K, :] = accs[i]

    def tri_copy(part, half, t, slot, other):
        return remote(
            tri_s.at[part, half], tri_rcv.at[slot, part, half],
            tri_ss.at[part, half, t], tri_rs.at[slot, part, half], r, other,
        )

    split = B > 1 and RPQ % B == 0

    def pass_on(t):
        if lead:
            head_wait(t * B)
            relay(t * B).start()

    halves = [mate(g * RPQ) // RPQ if split else g for g in range(Q)]
    if not split:
        if B > 1:
            loop(1, A, pass_on)
            arrive(1, False)
            for t in range(2, R):
                arrive(t, t % 2 == 1)
        else:
            loop(1, R, lambda t: arrive(t, False))
    for g, half in enumerate(halves):
        if split:
            start = g * (RPQ // B) if B > 1 and RPQ % B == 0 else 0
            if g == 0:
                if B > 1:
                    first = min(3, A)
                    loop(1, first, pass_on)
                    arrive(1, False)
                    loop(first, A, pass_on)
            for u in range(start, start + RPQ // B):
                for v in range(B):
                    if u:
                        arrive(u * B + v, v == 1)
        for part in range(2):
            partial(part, half)
            for t in range(1, Q):
                tri_copy(part, half, t, q, wrap(q + t, Q)).start()

    @pl.when(mine)
    def _():
        def col_wait(t):
            source = back(t)
            remote(
                dsend.at[0], drecv.at[source], dcol_ss.at[0], dcol_rs.at[source], source, q
            ).wait_recv()
        loop(1, R, col_wait)
        for t in range(1, Q):
            hand_on(t, wrap(q + t, Q)).start()

    for t in range(1, Q):
        other = wrap(q + t, Q)
        dn_copy(t, other, other).wait_recv()

    def complete(part, which):
        sums, weights = [], []
        for half in which:
            for t in range(1, Q):
                other = wrap(q + t, Q)
                tri_copy(part, half, t, other, other).wait_recv()
        for half in which:
            triangle = tri_s[part, half]
            for t in range(1, Q):
                triangle = triangle + tri_rcv[wrap(q + t, Q), part, half]
            sums.append(triangle)
            if part == 0:
                weights.append(dn[half])
            else:
                weights += [
                    dcol32[pl.ds(half * (K * pad) + j, K, stride=pad), :] for j in range(rows)
                ]
        weighted = jnp.concatenate(weights, axis=0)
        tri_hat, tri_inv = normalise(jnp.concatenate(sums, axis=0))
        d_tri = tri_inv * (weighted - tri_hat * mean_last(weighted * tri_hat))
        d_tri = d_tri.astype(BF16).astype(F32)
        for n, half in enumerate(which):
            d32[part, pl.ds(pl.multiple_of(half * M, 8), M), :] = d_tri[n * M : (n + 1) * M, :]
            if part == 0:
                hat2_s[half] = tri_hat[n * M : (n + 1) * M, :]

    def pull(part, which, accs):
        theirs = right32 if part == 0 else left32
        for half in which:
            def step(j, accs, half=half):
                block = theirs[pl.ds(pl.multiple_of((half * K + j) * K, 8), K), :]
                return tuple(
                    accs[i] + d32[part, pl.ds(half * M + i * K + j, 1), :] * block
                    for i in range(rows)
                )
            accs = lax.fori_loop(0, K, step, accs, unroll=8)
        return accs

    normed = gath[r]

    def settle(part, accs):
        grad = jnp.concatenate(accs, axis=0)
        first = (grad * coef[2 * part]).astype(BF16)
        second = (grad * coef[2 * part + 1]).astype(BF16)
        wide = dot(normed, jnp.concatenate([first, second], axis=-1), 0, 0)
        core_start(1 + part, wide[:, :H], wide[:, H:])
        return [first, second]

    def strips():
        @pl.when(jnp.logical_not(mine))
        def _():
            hand_on(0, r // RPQ).wait_recv()

        def widen_col(t):
            dcol32[pl.ds(pl.multiple_of(t * rows * pad, 8), rows * pad), :] = drecv[t].astype(F32)
        loop(0, R, widen_col)

    def gates():
        tri_norm = (hat2_s[q] * tg_ref[...] + tb_ref[...]).astype(BF16)
        update = dot(tri_norm, ow_ref[...])
        og = og_s[...]
        out_ref[...] = (og * update).astype(BF16)
        d_gate = (cot_ref[...].astype(F32) * update * og * (1.0 - og)).astype(BF16)
        core_start(0, dot(normed, d_gate, 0, 0), dot(tri_norm, dupd_s[...], 0, 0))
        return d_gate

    soon, late = halves[: Q - 1], halves[Q - 1 :]
    complete(0, soon)
    accs = pull(0, soon, zeros())
    complete(0, late)
    d_gate = gates()
    d_proj = settle(0, pull(0, late, accs))
    scatter_start(0)
    strips()
    complete(1, halves)
    d_proj += settle(1, pull(1, halves, zeros()))
    scatter_start(1)
    d_cat = jnp.concatenate(d_proj, axis=-1)
    d_normed = dot(d_cat, pw_ref[...], 1, 1) + dot(d_gate, gw_ref[...], 1, 1)
    pg_ref[...] = norm_back(d_normed * ng_ref[...], hat_s[...], inv_s[...])

    scatter_start(2)
    for g in range(3):
        spread_start(g)

    if B > 1:
        gather(1).wait_send()
        loop(1, A, lambda t: [gather(t * B + u).wait_send() for u in range(B)])
        if lead:
            loop(1, A, lambda t: [line_head(t * B).wait_send(), relay(t * B).wait_send()])
    else:
        loop(1, R, lambda t: gather(t).wait_send())
    for t in range(1, Q):
        other = wrap(q + t, Q)
        dn_copy(t, q, other).wait_send()
        for part in range(2):
            for half in range(Q):
                tri_copy(part, half, t, q, other).wait_send()
    each_target(lambda b, target: col_copy(b, target).wait_send())

    @pl.when(mine)
    def _():
        for t in range(1, Q):
            hand_on(t, wrap(q + t, Q)).wait_send()

    for g in range(3):
        spread_all(g).wait_recv()
        if not direct_out[g]:
            for t in range(1, Q):
                share(g, t, wrap(q + t, Q), q).start()
    for g in range(3):
        scatter_all(g).wait_send()
        spread_all(g).wait_send()
        if not direct_in[g]:
            for t in range(1, Q):
                core_copy(g, t, q, wrap(q + t, Q)).wait_send()
    for g in range(3):
        if not direct_out[g]:
            for t in range(1, Q):
                other = wrap(q + t, Q)
                share(g, t, other, other).wait_recv()
    gall_ref[...] = gfin[...]
    for g in range(3):
        if not direct_out[g]:
            for t in range(1, Q):
                share(g, t, wrap(q + t, Q), q).wait_send()


def finish(Q, R, piece, C, H, block_ref, grad_ref, gall_ref, out_ref, pg_ref, gp_ref, gg_ref, go_ref):
    out_ref[...] = block_ref[...]
    pg_ref[...] = grad_ref[...]
    targets = (
        (gg_ref, 0), (go_ref, 0), (gp_ref, 0), (gp_ref, H), (gp_ref, 2 * H), (gp_ref, 3 * H),
    )
    per = C // piece
    for t, (ref, col) in enumerate(targets):
        for p in range(per):
            whole = (t % 2) * per + p
            ref[p * piece : (p + 1) * piece, col : col + H] = gall_ref[t // 2, whole % Q * R + whole // Q].astype(F32)


def local(R, Q, pair_rep, cotangent, ng, nb, pw, gw, tg, tb, ow):
    rows, K, C = pair_rep.shape
    H = tg.shape[0]
    M = rows * K
    NP = R * Q
    RPQ = R // Q
    pad = -(-rows // 8) * 8
    piece = 2 * C // NP
    dma = pltpu.SemaphoreType.DMA
    vmem = pltpu.VMEM
    spec = pl.BlockSpec(memory_space=pltpu.VMEM)
    shapes = (
        jax.ShapeDtypeStruct((M, C), BF16),
        jax.ShapeDtypeStruct((M, C), F32),
        jax.ShapeDtypeStruct((3, NP, piece, H), BF16),
    )
    any_spec = pl.BlockSpec(memory_space=pl.ANY)
    parts = pl.pallas_call(
        functools.partial(kernel, R, Q, rows, K, H, C),
        out_shape=tuple(pltpu.VMEM(v.shape, v.dtype) for v in shapes),
        in_specs=[any_spec] * 9,
        out_specs=[spec] * 3,
        scratch_shapes=[
            vmem((M, C), BF16), vmem((M, C), BF16), vmem((1, C), F32), vmem((1, C), F32),
            vmem((C, 4 * H), BF16), vmem((C, C), BF16), vmem((1, H), F32), vmem((1, H), F32),
            vmem((H, C), BF16),
            vmem((R, M, C), BF16),
            vmem((R * M, H), F32),
            vmem((R * M, H), F32),
            vmem((4, M, H), F32),
            vmem((M, C), F32),
            vmem((M, C), F32),
            vmem((M, C), F32),
            vmem((M, C), BF16),
            vmem((Q, M, H), F32),
            vmem((Q, M, H), F32),
            vmem((2, Q, M, H), F32),
            vmem((Q, 2, Q, M, H), F32),
            vmem((2, Q * M, H), F32),
            vmem((RPQ, rows * pad, H), BF16),
            vmem((R, rows * pad, H), BF16),
            vmem((R * rows * pad, H), F32),
            vmem((3, Q, R, piece, H), BF16),
            vmem((3, Q, R, piece, H), BF16),
            vmem((3, R, piece, H), F32),
            vmem((3, NP, piece, H), BF16),
            vmem((3, NP, piece, H), BF16),
            vmem((3, NP, piece, H), BF16),
            dma((9,)),
            dma((4, R)), dma((2, R)),
            dma((2, Q, Q)), dma((Q, 2, Q)),
            dma((Q,)), dma((Q,)),
            dma((R,)), dma((R,)),
            pltpu.SemaphoreType.REGULAR, dma((Q,)), dma,
            dma((3, Q)), dma((3, Q)),
            dma((3,)), dma((3,)),
            dma((3,)), dma((3,)),
            dma((3, Q)), dma((3, Q)),
        ],
        compiler_params=pltpu.CompilerParams(
            collective_id=0, has_side_effects=True, vmem_limit_bytes=60 * 1024 * 1024
        ),
        name="triangle_step",
    )(
        pair_rep.reshape(M, C), cotangent.reshape(M, C), ng.reshape(1, C), nb.reshape(1, C),
        pw, gw, tg.reshape(1, H), tb.reshape(1, H), ow,
    )
    outs = pl.pallas_call(
        functools.partial(finish, Q, R, piece, C, H),
        out_shape=(
            shapes[0],
            shapes[1],
            jax.ShapeDtypeStruct((C, 4 * H), F32),
            jax.ShapeDtypeStruct((C, C), F32),
            jax.ShapeDtypeStruct((H, C), F32),
        ),
        in_specs=[spec] * 3,
        out_specs=[spec] * 5,
        compiler_params=pltpu.CompilerParams(vmem_limit_bytes=4 * 1024 * 1024),
        name="finish",
    )(*parts)
    return (
        outs[0].reshape(rows, K, C), outs[1].reshape(rows, K, C), outs[2], outs[3], outs[4],
    )


def solution(mesh):
    tile = P(("crop", "row"), "col", None)
    grad = P("crop", None)
    return jax.shard_map(
        functools.partial(local, mesh.shape["row"], mesh.shape["col"]),
        mesh=mesh,
        in_specs=(tile, tile, P(), P(), P(), P(), P(), P(), P()),
        out_specs=(tile, tile, grad, grad, grad),
        check_vma=False,
    )
```

```python
import functools

import jax
import jax.numpy as jnp
from jax import lax
from jax.experimental import pallas as pl
from jax.experimental.pallas import tpu as pltpu
from jax.sharding import PartitionSpec as P

F32 = jnp.float32
BF16 = jnp.bfloat16


def mean_last(values):
    return jnp.mean(values, axis=-1, keepdims=True)


def normalise(values):
    centred = values - mean_last(values)
    inverse = lax.rsqrt(mean_last(centred * centred) + 1e-05)
    return centred * inverse, inverse


def norm_back(weighted, scaled, inverse):
    return inverse * (weighted - mean_last(weighted) - scaled * mean_last(weighted * scaled))


def dot(a, b, ca=1, cb=0):
    return lax.dot_general(a, b, (((ca,), (cb,)), ((), ())), preferred_element_type=F32)


def kernel(
    R, Q, rows, K, H, C,
    x_hbm, cot_hbm, ng_hbm, nb_hbm, pw_hbm, gw_hbm, tg_hbm, tb_hbm, ow_hbm,
    out_ref, pg_ref, gall_ref,
    x_ref, cot_ref, ng_ref, nb_ref, pw_ref, gw_ref, tg_ref, tb_ref, ow_ref,
    gath, right32, left32, coef, og_s, hat_s, inv_s, dupd_s, dn,
    hat2_s, tri_s, tri_rcv, d32, dsend, drecv, dcol32,
    csend, crecv, gkeep, gsend, grecv, gfin,
    in_s, gath_ss, gath_rs, tri_ss, tri_rs, dn_ss, dn_rs, dcol_ss, dcol_rs,
    near, hand_ss, hand_rs, cs_ss, cs_rs, gs_ss, gs_rs, gf_ss, gf_rs, sh_ss, sh_rs,
):
    r = lax.axis_index("row")
    q = lax.axis_index("col")
    M = rows * K
    N = rows * R
    NP = R * Q
    RPQ = R // Q
    pad = -(-rows // 8) * 8
    me = q * R + r
    direct_in, direct_out = (False, False, False), (False, True, True)
    mine_pieces = pl.ds(q * R, R)

    def remote(src, dst, ss, rs, rr, qq):
        return pltpu.make_async_remote_copy(
            src_ref=src, dst_ref=dst, send_sem=ss, recv_sem=rs,
            device_id={"row": rr, "col": qq}, device_id_type=pl.DeviceIdType.MESH,
        )

    def loop(lo, hi, body):
        if hi - lo <= 16:
            for t in range(lo, hi):
                body(t)
            return

        def step(t, carry):
            body(t)
            return carry
        lax.fori_loop(lo, hi, step, 0)

    def wrap(value, size):
        return jnp.where(value >= size, value - size, value)

    def peer(t):
        rr, qq = wrap(r + t // Q, R), wrap(q + t % Q, Q)
        return rr, qq, rr * Q + qq

    B = 2 if R > 1 and not R & (R - 1) else 1

    def mate(t):
        if R & (R - 1):
            return lax.rem(r + t, R)
        out, bit = 0, 1
        while bit < R:
            out = out + bit * ((r // bit + t // bit) % 2)
            bit *= 2
        return out

    def back(t):
        return lax.rem(r + R - t, R) if R & (R - 1) else mate(t)

    barrier = pltpu.get_barrier_semaphore()

    A = R // B

    def signal(sem, rr, qq):
        pl.semaphore_signal(
            sem, inc=1, device_id={"row": rr, "col": qq}, device_id_type=pl.DeviceIdType.MESH
        )

    loop(1, A, lambda t: signal(barrier, mate(t * B), q))
    for t in range(1, B):
        signal(barrier, mate(t), q)
    for t in range(1, Q):
        signal(barrier, r, wrap(q + t, Q))

    fetch = [
        pltpu.make_async_copy(src, dst, in_s.at[n]) for n, (src, dst) in enumerate((
            (x_hbm, x_ref), (ng_hbm, ng_ref), (nb_hbm, nb_ref), (pw_hbm, pw_ref),
            (gw_hbm, gw_ref), (cot_hbm, cot_ref), (ow_hbm, ow_ref), (tg_hbm, tg_ref),
            (tb_hbm, tb_ref),
        ))
    ]
    for copy in fetch:
        copy.start()

    piece = 2 * C // NP
    per = NP // 2

    def core_copy(g, t, slot, other):
        return remote(
            csend.at[g, t], crecv.at[g, slot], cs_ss.at[g, t], cs_rs.at[g, slot], r, other
        )

    def core_start(g, first, second):
        both = (first, second)

        def part(qq, rr):
            whole = rr * Q + qq
            p = whole % per
            return both[whole // per][p * piece : (p + 1) * piece, :]
        if direct_in[g]:
            for rr in range(R):
                for qq in range(Q):
                    gsend[g, qq * R + rr] = part(qq, rr).astype(BF16)
            scatter_go(g)
            return
        for t in range(Q):
            other = wrap(q + t, Q)
            for rr in range(R):
                block = part(Q - 1, rr)
                for qq in range(Q - 1):
                    block = jnp.where(other == qq, part(qq, rr), block)
                if t:
                    csend[g, t, rr] = block.astype(BF16)
                else:
                    gkeep[g, rr] = block
            if t:
                core_copy(g, t, q, other).start()

    def targets(straight):
        return [(t, u) for t in range(R) for u in range(Q if straight else 1) if t or u]

    def scatter(g, t, u):
        rr, qq = (mate(t) if t else r), wrap(q + u, Q)
        return remote(
            gsend.at[g, qq * R + rr], grecv.at[g, me],
            gs_ss.at[g], gs_rs.at[g], rr, qq
        )

    def scatter_all(g):
        block = pl.ds(0, len(targets(direct_in[g])))
        return remote(
            gsend.at[g, block], grecv.at[g, block], gs_ss.at[g], gs_rs.at[g], r, q
        )

    def scatter_go(g):
        for t, u in targets(direct_in[g])[::-1]:
            scatter(g, t, u).start()
        grecv[g, me] = gsend[g, me]

    def scatter_start(g):
        if direct_in[g]:
            return
        total = gkeep[g]
        for t in range(1, Q):
            other = wrap(q + t, Q)
            core_copy(g, t, other, other).wait_recv()
            total = total + crecv[g, other].astype(F32)
        gsend[g, mine_pieces] = total.astype(BF16)
        scatter_go(g)

    def spread(g, t, u):
        rr, qq = (mate(t) if t else r), wrap(q + u, Q)
        return remote(gfin.at[g, me], gfin.at[g, me], gf_ss.at[g], gf_rs.at[g], rr, qq)

    def spread_all(g):
        block = pl.ds(0, len(targets(direct_out[g])))
        return remote(gfin.at[g, block], gfin.at[g, block], gf_ss.at[g], gf_rs.at[g], r, q)

    def spread_start(g):
        scatter_all(g).wait_recv()
        if direct_in[g]:
            parts = [grecv[g, p] for p in range(NP)]
        else:
            kept = grecv[g, mine_pieces]
            parts = [kept[p] for p in range(R)]
        total = parts[0].astype(F32)
        for p in parts[1:]:
            total = total + p.astype(F32)
        gfin[g, me] = (total / N).astype(BF16)
        for t, u in targets(direct_out[g]):
            spread(g, t, u).start()

    def share(g, t, other, slot):
        block = pl.ds(slot * R, R)
        return remote(
            gfin.at[g, block], gfin.at[g, block], sh_ss.at[g, t], sh_rs.at[g, slot], r, other
        )

    lead = M // 3 // 16 * 16 if B > 1 else 0
    head, rest, whole = pl.ds(0, lead), pl.ds(lead, M - lead), pl.ds(0, M)

    def block_copy(kind, src, t, lane, other):
        span = (head, rest, whole, head)[kind]
        return remote(
            gath.at[src, span], gath.at[src, span], gath_ss.at[kind, t], gath_rs.at[lane, src],
            other, q,
        )

    def line_head(t):
        return block_copy(0, r, t, 0, mate(t))

    def gather(t):
        return block_copy(2 if t_is_one(t) or not lead else 1, r, t, 1, mate(t))

    def t_is_one(t):
        return isinstance(t, int) and t == 1

    def relay(t):
        return block_copy(3, back(t), t, 0, mate(1))

    def head_wait(t):
        block_copy(0, back(t), t, 0, back(t)).wait_recv()

    def edge(gate, value):
        sig = jax.nn.sigmoid(gate)
        return (sig * value).astype(BF16).astype(F32), sig

    for n in range(3):
        fetch[n].wait()
    hat, inv = normalise(x_ref[...].astype(F32))
    normed = (hat * ng_ref[...] + nb_ref[...]).astype(BF16)
    hat_s[...] = hat
    inv_s[...] = jnp.broadcast_to(inv, hat.shape)
    gath[r] = normed

    for n in range(4, 9):
        fetch[n].wait()
    og = jax.nn.sigmoid(dot(normed, gw_ref[...]))
    og_s[...] = og
    d_update = (cot_ref[...].astype(F32) * og).astype(BF16)
    dupd_s[...] = d_update
    dn_own = dot(d_update, ow_ref[...], 1, 1) * tg_ref[...]
    dn_own = dn_own - mean_last(dn_own)
    dn[q] = dn_own
    for b in range(RPQ):
        parts = []
        for i in range(rows):
            block = dn_own[i * K + b * rows : i * K + (b + 1) * rows, :]
            if pad > rows:
                block = jnp.concatenate([block, jnp.zeros((pad - rows, H), F32)], axis=0)
            parts.append(block)
        dsend[b] = jnp.concatenate(parts, axis=0).astype(BF16)
    mine = r // RPQ == q

    @pl.when(mine)
    def _():
        drecv[r] = dsend[lax.rem(r, RPQ)]

    pl.semaphore_wait(barrier, A + B + Q - 3)
    for t in range(1, B):
        signal(near, mate(t), q)
    if B > 1:
        if lead:
            loop(1, A, lambda t: line_head(t * B).start())
        gather(1).start()
        pl.semaphore_wait(near, B - 1)
        loop(1, A, lambda t: [gather(t * B + u).start() for u in range(B)])
    else:
        loop(1, R, lambda t: gather(t).start())

    def dn_copy(t, slot, other):
        return remote(dn.at[q], dn.at[slot], dn_ss.at[t], dn_rs.at[slot], r, other)

    for t in range(1, Q):
        dn_copy(t, q, wrap(q + t, Q)).start()

    def each_target(act):
        def one(b):
            target = q * RPQ + b

            @pl.when(target != r)
            def _():
                act(b, target)
        loop(0, RPQ, one)

    def col_copy(b, target):
        return remote(dsend.at[b], drecv.at[r], dcol_ss.at[b], dcol_rs.at[r], target, q)

    each_target(lambda b, target: col_copy(b, target).start())

    def hand_on(t, other):
        return remote(drecv, drecv, hand_ss.at[t], hand_rs, r, other)

    own = pl.multiple_of(r * M, 8)
    fetch[3].wait()
    proj = dot(normed, pw_ref[...])
    vl, vr = proj[:, H : 2 * H], proj[:, 3 * H :]
    left_edge, sl = edge(proj[:, :H], vl)
    right_edge, sr = edge(proj[:, 2 * H : 3 * H], vr)
    left32[pl.ds(own, M), :] = left_edge
    right32[pl.ds(own, M), :] = right_edge
    coef[0] = vl * sl * (1.0 - sl)
    coef[1] = sl
    coef[2] = vr * sr * (1.0 - sr)
    coef[3] = sr
    def arrive(t, odd):
        source = back(t)
        block_copy(2 if t_is_one(t) or not lead else 1, source, t, 1, source).wait_recv()
        if lead and odd:
            block_copy(0, source, t, 0, mate(1)).wait_recv()
        proj = dot(gath[source], pw_ref[...])
        place = pl.ds(pl.multiple_of(source * M, 8), M)
        left32[place, :] = edge(proj[:, :H], proj[:, H : 2 * H])[0]
        right32[place, :] = edge(proj[:, 2 * H : 3 * H], proj[:, 3 * H :])[0]
    def zeros():
        return tuple(jnp.zeros((K, H), F32) for _ in range(rows))

    def partial(part, half):
        ours, theirs = (left32, right32) if part == 0 else (right32, left32)
        base = half * (K * K)

        def step(k, accs):
            block = theirs[pl.ds(base + k, K, stride=K), :]
            return tuple(
                accs[i] + ours[pl.ds(own + i * K + k, 1), :] * block for i in range(rows)
            )
        accs = lax.fori_loop(0, K, step, zeros(), unroll=8)
        for i in range(rows):
            tri_s[part, half, i * K : (i + 1) * K, :] = accs[i]

    def tri_copy(part, half, t, slot, other):
        return remote(
            tri_s.at[part, half], tri_rcv.at[slot, part, half],
            tri_ss.at[part, half, t], tri_rs.at[slot, part, half], r, other,
        )

    split = B > 1 and RPQ % B == 0

    def pass_on(t):
        if lead:
            head_wait(t * B)
            relay(t * B).start()

    halves = [mate(g * RPQ) // RPQ if split else g for g in range(Q)]
    if not split:
        if B > 1:
            loop(1, A, pass_on)
            arrive(1, False)
            for t in range(2, R):
                arrive(t, t % 2 == 1)
        else:
            loop(1, R, lambda t: arrive(t, False))
    for g, half in enumerate(halves):
        if split:
            start = g * (RPQ // B) if B > 1 and RPQ % B == 0 else 0
            if g == 0:
                if B > 1:
                    first = min(3, A)
                    loop(1, first, pass_on)
                    arrive(1, False)
                    loop(first, A, pass_on)
            for u in range(start, start + RPQ // B):
                for v in range(B):
                    if u:
                        arrive(u * B + v, v == 1)
        for part in range(2):
            partial(part, half)
            for t in range(1, Q):
                tri_copy(part, half, t, q, wrap(q + t, Q)).start()

    @pl.when(mine)
    def _():
        def col_wait(t):
            source = back(t)
            remote(
                dsend.at[0], drecv.at[source], dcol_ss.at[0], dcol_rs.at[source], source, q
            ).wait_recv()
        loop(1, R, col_wait)
        for t in range(1, Q):
            hand_on(t, wrap(q + t, Q)).start()

    for t in range(1, Q):
        other = wrap(q + t, Q)
        dn_copy(t, other, other).wait_recv()

    def complete(part, which):
        sums, weights = [], []
        for half in which:
            for t in range(1, Q):
                other = wrap(q + t, Q)
                tri_copy(part, half, t, other, other).wait_recv()
        for half in which:
            triangle = tri_s[part, half]
            for t in range(1, Q):
                triangle = triangle + tri_rcv[wrap(q + t, Q), part, half]
            sums.append(triangle)
            if part == 0:
                weights.append(dn[half])
            else:
                weights += [
                    dcol32[pl.ds(half * (K * pad) + j, K, stride=pad), :] for j in range(rows)
                ]
        weighted = jnp.concatenate(weights, axis=0)
        tri_hat, tri_inv = normalise(jnp.concatenate(sums, axis=0))
        d_tri = tri_inv * (weighted - tri_hat * mean_last(weighted * tri_hat))
        d_tri = d_tri.astype(BF16).astype(F32)
        for n, half in enumerate(which):
            d32[part, pl.ds(pl.multiple_of(half * M, 8), M), :] = d_tri[n * M : (n + 1) * M, :]
            if part == 0:
                hat2_s[half] = tri_hat[n * M : (n + 1) * M, :]

    def pull(part, which, accs):
        theirs = right32 if part == 0 else left32
        for half in which:
            def step(j, accs, half=half):
                block = theirs[pl.ds(pl.multiple_of((half * K + j) * K, 8), K), :]
                return tuple(
                    accs[i] + d32[part, pl.ds(half * M + i * K + j, 1), :] * block
                    for i in range(rows)
                )
            accs = lax.fori_loop(0, K, step, accs, unroll=8)
        return accs

    normed = gath[r]

    def settle(part, accs):
        grad = jnp.concatenate(accs, axis=0)
        first = (grad * coef[2 * part]).astype(BF16)
        second = (grad * coef[2 * part + 1]).astype(BF16)
        wide = dot(normed, jnp.concatenate([first, second], axis=-1), 0, 0)
        core_start(1 + part, wide[:, :H], wide[:, H:])
        return [first, second]

    def strips():
        @pl.when(jnp.logical_not(mine))
        def _():
            hand_on(0, r // RPQ).wait_recv()

        def widen_col(t):
            dcol32[pl.ds(pl.multiple_of(t * rows * pad, 8), rows * pad), :] = drecv[t].astype(F32)
        loop(0, R, widen_col)

    def gates():
        tri_norm = (hat2_s[q] * tg_ref[...] + tb_ref[...]).astype(BF16)
        update = dot(tri_norm, ow_ref[...])
        og = og_s[...]
        out_ref[...] = (og * update).astype(BF16)
        d_gate = (cot_ref[...].astype(F32) * update * og * (1.0 - og)).astype(BF16)
        core_start(0, dot(normed, d_gate, 0, 0), dot(tri_norm, dupd_s[...], 0, 0))
        return d_gate

    soon, late = halves[: Q - 1], halves[Q - 1 :]
    complete(0, soon)
    accs = pull(0, soon, zeros())
    complete(0, late)
    d_gate = gates()
    d_proj = settle(0, pull(0, late, accs))
    scatter_start(0)
    strips()
    complete(1, soon)
    accs = pull(1, soon, zeros())
    scatter_start(1)
    complete(1, late)
    d_proj += settle(1, pull(1, late, accs))
    d_cat = jnp.concatenate(d_proj, axis=-1)
    d_normed = dot(d_cat, pw_ref[...], 1, 1) + dot(d_gate, gw_ref[...], 1, 1)
    pg_ref[...] = norm_back(d_normed * ng_ref[...], hat_s[...], inv_s[...])

    scatter_start(2)
    for g in range(3):
        spread_start(g)

    if B > 1:
        gather(1).wait_send()
        loop(1, A, lambda t: [gather(t * B + u).wait_send() for u in range(B)])
        if lead:
            loop(1, A, lambda t: [line_head(t * B).wait_send(), relay(t * B).wait_send()])
    else:
        loop(1, R, lambda t: gather(t).wait_send())
    for t in range(1, Q):
        other = wrap(q + t, Q)
        dn_copy(t, q, other).wait_send()
        for part in range(2):
            for half in range(Q):
                tri_copy(part, half, t, q, other).wait_send()
    each_target(lambda b, target: col_copy(b, target).wait_send())

    @pl.when(mine)
    def _():
        for t in range(1, Q):
            hand_on(t, wrap(q + t, Q)).wait_send()

    for g in range(3):
        spread_all(g).wait_recv()
        if not direct_out[g]:
            for t in range(1, Q):
                share(g, t, wrap(q + t, Q), q).start()
    for g in range(3):
        scatter_all(g).wait_send()
        spread_all(g).wait_send()
        if not direct_in[g]:
            for t in range(1, Q):
                core_copy(g, t, q, wrap(q + t, Q)).wait_send()
    for g in range(3):
        if not direct_out[g]:
            for t in range(1, Q):
                other = wrap(q + t, Q)
                share(g, t, other, other).wait_recv()
    gall_ref[...] = gfin[...]
    for g in range(3):
        if not direct_out[g]:
            for t in range(1, Q):
                share(g, t, wrap(q + t, Q), q).wait_send()


def finish(Q, R, piece, C, H, block_ref, grad_ref, gall_ref, out_ref, pg_ref, gp_ref, gg_ref, go_ref):
    out_ref[...] = block_ref[...]
    pg_ref[...] = grad_ref[...]
    targets = (
        (gg_ref, 0), (go_ref, 0), (gp_ref, 0), (gp_ref, H), (gp_ref, 2 * H), (gp_ref, 3 * H),
    )
    per = C // piece
    for t, (ref, col) in enumerate(targets):
        for p in range(per):
            whole = (t % 2) * per + p
            ref[p * piece : (p + 1) * piece, col : col + H] = gall_ref[t // 2, whole % Q * R + whole // Q].astype(F32)


def local(R, Q, pair_rep, cotangent, ng, nb, pw, gw, tg, tb, ow):
    rows, K, C = pair_rep.shape
    H = tg.shape[0]
    M = rows * K
    NP = R * Q
    RPQ = R // Q
    pad = -(-rows // 8) * 8
    piece = 2 * C // NP
    dma = pltpu.SemaphoreType.DMA
    vmem = pltpu.VMEM
    spec = pl.BlockSpec(memory_space=pltpu.VMEM)
    shapes = (
        jax.ShapeDtypeStruct((M, C), BF16),
        jax.ShapeDtypeStruct((M, C), F32),
        jax.ShapeDtypeStruct((3, NP, piece, H), BF16),
    )
    any_spec = pl.BlockSpec(memory_space=pl.ANY)
    parts = pl.pallas_call(
        functools.partial(kernel, R, Q, rows, K, H, C),
        out_shape=tuple(pltpu.VMEM(v.shape, v.dtype) for v in shapes),
        in_specs=[any_spec] * 9,
        out_specs=[spec] * 3,
        scratch_shapes=[
            vmem((M, C), BF16), vmem((M, C), BF16), vmem((1, C), F32), vmem((1, C), F32),
            vmem((C, 4 * H), BF16), vmem((C, C), BF16), vmem((1, H), F32), vmem((1, H), F32),
            vmem((H, C), BF16),
            vmem((R, M, C), BF16),
            vmem((R * M, H), F32),
            vmem((R * M, H), F32),
            vmem((4, M, H), F32),
            vmem((M, C), F32),
            vmem((M, C), F32),
            vmem((M, C), F32),
            vmem((M, C), BF16),
            vmem((Q, M, H), F32),
            vmem((Q, M, H), F32),
            vmem((2, Q, M, H), F32),
            vmem((Q, 2, Q, M, H), F32),
            vmem((2, Q * M, H), F32),
            vmem((RPQ, rows * pad, H), BF16),
            vmem((R, rows * pad, H), BF16),
            vmem((R * rows * pad, H), F32),
            vmem((3, Q, R, piece, H), BF16),
            vmem((3, Q, R, piece, H), BF16),
            vmem((3, R, piece, H), F32),
            vmem((3, NP, piece, H), BF16),
            vmem((3, NP, piece, H), BF16),
            vmem((3, NP, piece, H), BF16),
            dma((9,)),
            dma((4, R)), dma((2, R)),
            dma((2, Q, Q)), dma((Q, 2, Q)),
            dma((Q,)), dma((Q,)),
            dma((R,)), dma((R,)),
            pltpu.SemaphoreType.REGULAR, dma((Q,)), dma,
            dma((3, Q)), dma((3, Q)),
            dma((3,)), dma((3,)),
            dma((3,)), dma((3,)),
            dma((3, Q)), dma((3, Q)),
        ],
        compiler_params=pltpu.CompilerParams(
            collective_id=0, has_side_effects=True, vmem_limit_bytes=60 * 1024 * 1024
        ),
        name="triangle_step",
    )(
        pair_rep.reshape(M, C), cotangent.reshape(M, C), ng.reshape(1, C), nb.reshape(1, C),
        pw, gw, tg.reshape(1, H), tb.reshape(1, H), ow,
    )
    outs = pl.pallas_call(
        functools.partial(finish, Q, R, piece, C, H),
        out_shape=(
            shapes[0],
            shapes[1],
            jax.ShapeDtypeStruct((C, 4 * H), F32),
            jax.ShapeDtypeStruct((C, C), F32),
            jax.ShapeDtypeStruct((H, C), F32),
        ),
        in_specs=[spec] * 3,
        out_specs=[spec] * 5,
        compiler_params=pltpu.CompilerParams(vmem_limit_bytes=4 * 1024 * 1024),
        name="finish",
    )(*parts)
    return (
        outs[0].reshape(rows, K, C), outs[1].reshape(rows, K, C), outs[2], outs[3], outs[4],
    )


def solution(mesh):
    tile = P(("crop", "row"), "col", None)
    grad = P("crop", None)
    return jax.shard_map(
        functools.partial(local, mesh.shape["row"], mesh.shape["col"]),
        mesh=mesh,
        in_specs=(tile, tile, P(), P(), P(), P(), P(), P(), P()),
        out_specs=(tile, tile, grad, grad, grad),
        check_vma=False,
    )
```

```python
import functools

import jax
import jax.numpy as jnp
from jax import lax
from jax.experimental import pallas as pl
from jax.experimental.pallas import tpu as pltpu
from jax.sharding import PartitionSpec as P

F32 = jnp.float32
BF16 = jnp.bfloat16


def mean_last(values):
    return jnp.mean(values, axis=-1, keepdims=True)


def normalise(values):
    centred = values - mean_last(values)
    inverse = lax.rsqrt(mean_last(centred * centred) + 1e-05)
    return centred * inverse, inverse


def norm_back(weighted, scaled, inverse):
    return inverse * (weighted - mean_last(weighted) - scaled * mean_last(weighted * scaled))


def dot(a, b, ca=1, cb=0):
    return lax.dot_general(a, b, (((ca,), (cb,)), ((), ())), preferred_element_type=F32)


def kernel(
    R, Q, rows, K, H, C,
    x_hbm, cot_hbm, ng_hbm, nb_hbm, pw_hbm, gw_hbm, tg_hbm, tb_hbm, ow_hbm,
    out_ref, pg_ref, gall_ref,
    x_ref, cot_ref, ng_ref, nb_ref, pw_ref, gw_ref, tg_ref, tb_ref, ow_ref,
    gath, right32, left32, coef, og_s, hat_s, inv_s, dupd_s, dn,
    hat2_s, tri_s, tri_rcv, d32, dsend, drecv, dcol32,
    csend, crecv, gkeep, gsend, grecv, gfin,
    in_s, gath_ss, gath_rs, tri_ss, tri_rs, dn_ss, dn_rs, dcol_ss, dcol_rs,
    near, hand_ss, hand_rs, cs_ss, cs_rs, gs_ss, gs_rs, gf_ss, gf_rs, sh_ss, sh_rs,
):
    r = lax.axis_index("row")
    q = lax.axis_index("col")
    M = rows * K
    N = rows * R
    NP = R * Q
    RPQ = R // Q
    pad = -(-rows // 8) * 8
    me = q * R + r
    direct_in, direct_out = (False, False, False), (False, True, True)
    mine_pieces = pl.ds(q * R, R)

    def remote(src, dst, ss, rs, rr, qq):
        return pltpu.make_async_remote_copy(
            src_ref=src, dst_ref=dst, send_sem=ss, recv_sem=rs,
            device_id={"row": rr, "col": qq}, device_id_type=pl.DeviceIdType.MESH,
        )

    def loop(lo, hi, body):
        if hi - lo <= 16:
            for t in range(lo, hi):
                body(t)
            return

        def step(t, carry):
            body(t)
            return carry
        lax.fori_loop(lo, hi, step, 0)

    def wrap(value, size):
        return jnp.where(value >= size, value - size, value)

    def peer(t):
        rr, qq = wrap(r + t // Q, R), wrap(q + t % Q, Q)
        return rr, qq, rr * Q + qq

    B = 2 if R > 1 and not R & (R - 1) else 1

    def mate(t):
        if R & (R - 1):
            return lax.rem(r + t, R)
        out, bit = 0, 1
        while bit < R:
            out = out + bit * ((r // bit + t // bit) % 2)
            bit *= 2
        return out

    def back(t):
        return lax.rem(r + R - t, R) if R & (R - 1) else mate(t)

    barrier = pltpu.get_barrier_semaphore()

    A = R // B

    def signal(sem, rr, qq):
        pl.semaphore_signal(
            sem, inc=1, device_id={"row": rr, "col": qq}, device_id_type=pl.DeviceIdType.MESH
        )

    loop(1, A, lambda t: signal(barrier, mate(t * B), q))
    for t in range(1, B):
        signal(barrier, mate(t), q)
    for t in range(1, Q):
        signal(barrier, r, wrap(q + t, Q))

    fetch = [
        pltpu.make_async_copy(src, dst, in_s.at[n]) for n, (src, dst) in enumerate((
            (x_hbm, x_ref), (ng_hbm, ng_ref), (nb_hbm, nb_ref), (pw_hbm, pw_ref),
            (gw_hbm, gw_ref), (cot_hbm, cot_ref), (ow_hbm, ow_ref), (tg_hbm, tg_ref),
            (tb_hbm, tb_ref),
        ))
    ]
    for copy in fetch:
        copy.start()

    piece = 2 * C // NP
    per = NP // 2

    def core_copy(g, t, slot, other):
        return remote(
            csend.at[g, t], crecv.at[g, slot], cs_ss.at[g, t], cs_rs.at[g, slot], r, other
        )

    def core_start(g, first, second):
        both = (first, second)

        def part(qq, rr):
            whole = rr * Q + qq
            p = whole % per
            return both[whole // per][p * piece : (p + 1) * piece, :]
        if direct_in[g]:
            for rr in range(R):
                for qq in range(Q):
                    gsend[g, qq * R + rr] = part(qq, rr).astype(BF16)
            scatter_go(g)
            return
        for t in range(Q):
            other = wrap(q + t, Q)
            for rr in range(R):
                block = part(Q - 1, rr)
                for qq in range(Q - 1):
                    block = jnp.where(other == qq, part(qq, rr), block)
                if t:
                    csend[g, t, rr] = block.astype(BF16)
                else:
                    gkeep[g, rr] = block
            if t:
                core_copy(g, t, q, other).start()

    def targets(straight):
        return [(t, u) for t in range(R) for u in range(Q if straight else 1) if t or u]

    def scatter(g, t, u):
        rr, qq = (mate(t) if t else r), wrap(q + u, Q)
        return remote(
            gsend.at[g, qq * R + rr], grecv.at[g, me],
            gs_ss.at[g], gs_rs.at[g], rr, qq
        )

    def scatter_all(g):
        block = pl.ds(0, len(targets(direct_in[g])))
        return remote(
            gsend.at[g, block], grecv.at[g, block], gs_ss.at[g], gs_rs.at[g], r, q
        )

    def scatter_go(g):
        for t, u in targets(direct_in[g])[::-1]:
            scatter(g, t, u).start()
        grecv[g, me] = gsend[g, me]

    def scatter_start(g):
        if direct_in[g]:
            return
        total = gkeep[g]
        for t in range(1, Q):
            other = wrap(q + t, Q)
            core_copy(g, t, other, other).wait_recv()
            total = total + crecv[g, other].astype(F32)
        gsend[g, mine_pieces] = total.astype(BF16)
        scatter_go(g)

    def spread(g, t, u):
        rr, qq = (mate(t) if t else r), wrap(q + u, Q)
        return remote(gfin.at[g, me], gfin.at[g, me], gf_ss.at[g], gf_rs.at[g], rr, qq)

    def spread_all(g):
        block = pl.ds(0, len(targets(direct_out[g])))
        return remote(gfin.at[g, block], gfin.at[g, block], gf_ss.at[g], gf_rs.at[g], r, q)

    def spread_start(g):
        scatter_all(g).wait_recv()
        if direct_in[g]:
            parts = [grecv[g, p] for p in range(NP)]
        else:
            kept = grecv[g, mine_pieces]
            parts = [kept[p] for p in range(R)]
        total = parts[0].astype(F32)
        for p in parts[1:]:
            total = total + p.astype(F32)
        gfin[g, me] = (total / N).astype(BF16)
        for t, u in targets(direct_out[g]):
            spread(g, t, u).start()

    def share(g, t, other, slot):
        block = pl.ds(slot * R, R)
        return remote(
            gfin.at[g, block], gfin.at[g, block], sh_ss.at[g, t], sh_rs.at[g, slot], r, other
        )

    lead = 5 * M // 9 // 16 * 16 if B > 1 else 0
    far = range(max(B, R // 2), R, B) if lead else ()
    head, rest, whole = pl.ds(0, lead), pl.ds(lead, M - lead), pl.ds(0, M)

    def block_copy(kind, src, t, lane, other):
        span = (head, rest, whole, head)[kind]
        return remote(
            gath.at[src, span], gath.at[src, span], gath_ss.at[kind, t], gath_rs.at[lane, src],
            other, q,
        )

    def line_head(t):
        return block_copy(0, r, t, 0, mate(t))

    def gather(t):
        return block_copy(1 if parted(t) else 2, r, t, 1, mate(t))

    def parted(t):
        return bool(far) and t >= far[0]

    def relay(t):
        return block_copy(3, back(t), t, 0, mate(1))

    def head_wait(t):
        block_copy(0, back(t), t, 0, back(t)).wait_recv()

    def edge(gate, value):
        sig = jax.nn.sigmoid(gate)
        return (sig * value).astype(BF16).astype(F32), sig

    for n in range(3):
        fetch[n].wait()
    hat, inv = normalise(x_ref[...].astype(F32))
    normed = (hat * ng_ref[...] + nb_ref[...]).astype(BF16)
    hat_s[...] = hat
    inv_s[...] = jnp.broadcast_to(inv, hat.shape)
    gath[r] = normed

    for n in range(4, 9):
        fetch[n].wait()
    og = jax.nn.sigmoid(dot(normed, gw_ref[...]))
    og_s[...] = og
    d_update = (cot_ref[...].astype(F32) * og).astype(BF16)
    dupd_s[...] = d_update
    dn_own = dot(d_update, ow_ref[...], 1, 1) * tg_ref[...]
    dn_own = dn_own - mean_last(dn_own)
    dn[q] = dn_own
    for b in range(RPQ):
        parts = []
        for i in range(rows):
            block = dn_own[i * K + b * rows : i * K + (b + 1) * rows, :]
            if pad > rows:
                block = jnp.concatenate([block, jnp.zeros((pad - rows, H), F32)], axis=0)
            parts.append(block)
        dsend[b] = jnp.concatenate(parts, axis=0).astype(BF16)
    mine = r // RPQ == q

    @pl.when(mine)
    def _():
        drecv[r] = dsend[lax.rem(r, RPQ)]

    pl.semaphore_wait(barrier, A + B + Q - 3)
    for t in range(1, B):
        signal(near, mate(t), q)
    if B > 1:
        for t in far:
            line_head(t).start()
        gather(1).start()
        pl.semaphore_wait(near, B - 1)
        for t in range(B, R):
            gather(t).start()
    else:
        loop(1, R, lambda t: gather(t).start())

    def dn_copy(t, slot, other):
        return remote(dn.at[q], dn.at[slot], dn_ss.at[t], dn_rs.at[slot], r, other)

    for t in range(1, Q):
        dn_copy(t, q, wrap(q + t, Q)).start()

    def each_target(act):
        def one(b):
            target = q * RPQ + b

            @pl.when(target != r)
            def _():
                act(b, target)
        loop(0, RPQ, one)

    def col_copy(b, target):
        return remote(dsend.at[b], drecv.at[r], dcol_ss.at[b], dcol_rs.at[r], target, q)

    each_target(lambda b, target: col_copy(b, target).start())

    def hand_on(t, other):
        return remote(drecv, drecv, hand_ss.at[t], hand_rs, r, other)

    own = pl.multiple_of(r * M, 8)
    fetch[3].wait()
    proj = dot(normed, pw_ref[...])
    vl, vr = proj[:, H : 2 * H], proj[:, 3 * H :]
    left_edge, sl = edge(proj[:, :H], vl)
    right_edge, sr = edge(proj[:, 2 * H : 3 * H], vr)
    left32[pl.ds(own, M), :] = left_edge
    right32[pl.ds(own, M), :] = right_edge
    coef[0] = vl * sl * (1.0 - sl)
    coef[1] = sl
    coef[2] = vr * sr * (1.0 - sr)
    coef[3] = sr
    def arrive(t, odd):
        source = back(t)
        block_copy(1 if parted(t) else 2, source, t, 1, source).wait_recv()
        if parted(t) and odd:
            block_copy(0, source, t, 0, mate(1)).wait_recv()
        proj = dot(gath[source], pw_ref[...])
        place = pl.ds(pl.multiple_of(source * M, 8), M)
        left32[place, :] = edge(proj[:, :H], proj[:, H : 2 * H])[0]
        right32[place, :] = edge(proj[:, 2 * H : 3 * H], proj[:, 3 * H :])[0]
    def zeros():
        return tuple(jnp.zeros((K, H), F32) for _ in range(rows))

    def partial(part, half):
        ours, theirs = (left32, right32) if part == 0 else (right32, left32)
        base = half * (K * K)

        def step(k, accs):
            block = theirs[pl.ds(base + k, K, stride=K), :]
            return tuple(
                accs[i] + ours[pl.ds(own + i * K + k, 1), :] * block for i in range(rows)
            )
        accs = lax.fori_loop(0, K, step, zeros(), unroll=8)
        for i in range(rows):
            tri_s[part, half, i * K : (i + 1) * K, :] = accs[i]

    def tri_copy(part, half, t, slot, other):
        return remote(
            tri_s.at[part, half], tri_rcv.at[slot, part, half],
            tri_ss.at[part, half, t], tri_rs.at[slot, part, half], r, other,
        )

    split = B > 1 and RPQ % B == 0

    def pass_on(t):
        if parted(t * B):
            head_wait(t * B)
            relay(t * B).start()

    halves = [mate(g * RPQ) // RPQ if split else g for g in range(Q)]
    if not split:
        if B > 1:
            [pass_on(t) for t in range(1, A)]
            arrive(1, False)
            for t in range(2, R):
                arrive(t, t % 2 == 1)
        else:
            loop(1, R, lambda t: arrive(t, False))
    for g, half in enumerate(halves):
        if split:
            start = g * (RPQ // B) if B > 1 and RPQ % B == 0 else 0
            if g == 0:
                if B > 1:
                    first = min(3, A)
                    [pass_on(t) for t in range(1, first)]
                    arrive(1, False)
                    [pass_on(t) for t in range(first, A)]
            for u in range(start, start + RPQ // B):
                for v in range(B):
                    if u:
                        arrive(u * B + v, v == 1)
        for part in range(2):
            partial(part, half)
            for t in range(1, Q):
                tri_copy(part, half, t, q, wrap(q + t, Q)).start()

    @pl.when(mine)
    def _():
        def col_wait(t):
            source = back(t)
            remote(
                dsend.at[0], drecv.at[source], dcol_ss.at[0], dcol_rs.at[source], source, q
            ).wait_recv()
        loop(1, R, col_wait)
        for t in range(1, Q):
            hand_on(t, wrap(q + t, Q)).start()

    for t in range(1, Q):
        other = wrap(q + t, Q)
        dn_copy(t, other, other).wait_recv()

    def complete(part, which):
        sums, weights = [], []
        for half in which:
            for t in range(1, Q):
                other = wrap(q + t, Q)
                tri_copy(part, half, t, other, other).wait_recv()
        for half in which:
            triangle = tri_s[part, half]
            for t in range(1, Q):
                triangle = triangle + tri_rcv[wrap(q + t, Q), part, half]
            sums.append(triangle)
            if part == 0:
                weights.append(dn[half])
            else:
                weights += [
                    dcol32[pl.ds(half * (K * pad) + j, K, stride=pad), :] for j in range(rows)
                ]
        weighted = jnp.concatenate(weights, axis=0)
        tri_hat, tri_inv = normalise(jnp.concatenate(sums, axis=0))
        d_tri = tri_inv * (weighted - tri_hat * mean_last(weighted * tri_hat))
        d_tri = d_tri.astype(BF16).astype(F32)
        for n, half in enumerate(which):
            d32[part, pl.ds(pl.multiple_of(half * M, 8), M), :] = d_tri[n * M : (n + 1) * M, :]
            if part == 0:
                hat2_s[half] = tri_hat[n * M : (n + 1) * M, :]

    def pull(part, which, accs):
        theirs = right32 if part == 0 else left32
        for half in which:
            def step(j, accs, half=half):
                block = theirs[pl.ds(pl.multiple_of((half * K + j) * K, 8), K), :]
                return tuple(
                    accs[i] + d32[part, pl.ds(half * M + i * K + j, 1), :] * block
                    for i in range(rows)
                )
            accs = lax.fori_loop(0, K, step, accs, unroll=8)
        return accs

    normed = gath[r]

    def settle(part, accs):
        grad = jnp.concatenate(accs, axis=0)
        first = (grad * coef[2 * part]).astype(BF16)
        second = (grad * coef[2 * part + 1]).astype(BF16)
        wide = dot(normed, jnp.concatenate([first, second], axis=-1), 0, 0)
        core_start(1 + part, wide[:, :H], wide[:, H:])
        return [first, second]

    def strips():
        @pl.when(jnp.logical_not(mine))
        def _():
            hand_on(0, r // RPQ).wait_recv()

        def widen_col(t):
            dcol32[pl.ds(pl.multiple_of(t * rows * pad, 8), rows * pad), :] = drecv[t].astype(F32)
        loop(0, R, widen_col)

    def gates():
        tri_norm = (hat2_s[q] * tg_ref[...] + tb_ref[...]).astype(BF16)
        update = dot(tri_norm, ow_ref[...])
        og = og_s[...]
        out_ref[...] = (og * update).astype(BF16)
        d_gate = (cot_ref[...].astype(F32) * update * og * (1.0 - og)).astype(BF16)
        core_start(0, dot(normed, d_gate, 0, 0), dot(tri_norm, dupd_s[...], 0, 0))
        return d_gate

    soon, late = halves[: Q - 1], halves[Q - 1 :]
    complete(0, soon)
    accs = pull(0, soon, zeros())
    complete(0, late)
    d_gate = gates()
    d_proj = settle(0, pull(0, late, accs))
    scatter_start(0)
    strips()
    complete(1, soon)
    accs = pull(1, soon, zeros())
    scatter_start(1)
    complete(1, late)
    d_proj += settle(1, pull(1, late, accs))
    d_cat = jnp.concatenate(d_proj, axis=-1)
    d_normed = dot(d_cat, pw_ref[...], 1, 1) + dot(d_gate, gw_ref[...], 1, 1)
    pg_ref[...] = norm_back(d_normed * ng_ref[...], hat_s[...], inv_s[...])

    scatter_start(2)
    for g in range(3):
        spread_start(g)

    if B > 1:
        gather(1).wait_send()
        for t in range(B, R):
            gather(t).wait_send()
        for t in far:
            line_head(t).wait_send()
            relay(t).wait_send()
    else:
        loop(1, R, lambda t: gather(t).wait_send())
    for t in range(1, Q):
        other = wrap(q + t, Q)
        dn_copy(t, q, other).wait_send()
        for part in range(2):
            for half in range(Q):
                tri_copy(part, half, t, q, other).wait_send()
    each_target(lambda b, target: col_copy(b, target).wait_send())

    @pl.when(mine)
    def _():
        for t in range(1, Q):
            hand_on(t, wrap(q + t, Q)).wait_send()

    for g in range(3):
        spread_all(g).wait_recv()
        if not direct_out[g]:
            for t in range(1, Q):
                share(g, t, wrap(q + t, Q), q).start()
    for g in range(3):
        scatter_all(g).wait_send()
        spread_all(g).wait_send()
        if not direct_in[g]:
            for t in range(1, Q):
                core_copy(g, t, q, wrap(q + t, Q)).wait_send()
    for g in range(3):
        if not direct_out[g]:
            for t in range(1, Q):
                other = wrap(q + t, Q)
                share(g, t, other, other).wait_recv()
    gall_ref[...] = gfin[...]
    for g in range(3):
        if not direct_out[g]:
            for t in range(1, Q):
                share(g, t, wrap(q + t, Q), q).wait_send()


def finish(Q, R, piece, C, H, block_ref, grad_ref, gall_ref, out_ref, pg_ref, gp_ref, gg_ref, go_ref):
    out_ref[...] = block_ref[...]
    pg_ref[...] = grad_ref[...]
    targets = (
        (gg_ref, 0), (go_ref, 0), (gp_ref, 0), (gp_ref, H), (gp_ref, 2 * H), (gp_ref, 3 * H),
    )
    per = C // piece
    for t, (ref, col) in enumerate(targets):
        for p in range(per):
            whole = (t % 2) * per + p
            ref[p * piece : (p + 1) * piece, col : col + H] = gall_ref[t // 2, whole % Q * R + whole // Q].astype(F32)


def local(R, Q, pair_rep, cotangent, ng, nb, pw, gw, tg, tb, ow):
    rows, K, C = pair_rep.shape
    H = tg.shape[0]
    M = rows * K
    NP = R * Q
    RPQ = R // Q
    pad = -(-rows // 8) * 8
    piece = 2 * C // NP
    dma = pltpu.SemaphoreType.DMA
    vmem = pltpu.VMEM
    spec = pl.BlockSpec(memory_space=pltpu.VMEM)
    shapes = (
        jax.ShapeDtypeStruct((M, C), BF16),
        jax.ShapeDtypeStruct((M, C), F32),
        jax.ShapeDtypeStruct((3, NP, piece, H), BF16),
    )
    any_spec = pl.BlockSpec(memory_space=pl.ANY)
    parts = pl.pallas_call(
        functools.partial(kernel, R, Q, rows, K, H, C),
        out_shape=tuple(pltpu.VMEM(v.shape, v.dtype) for v in shapes),
        in_specs=[any_spec] * 9,
        out_specs=[spec] * 3,
        scratch_shapes=[
            vmem((M, C), BF16), vmem((M, C), BF16), vmem((1, C), F32), vmem((1, C), F32),
            vmem((C, 4 * H), BF16), vmem((C, C), BF16), vmem((1, H), F32), vmem((1, H), F32),
            vmem((H, C), BF16),
            vmem((R, M, C), BF16),
            vmem((R * M, H), F32),
            vmem((R * M, H), F32),
            vmem((4, M, H), F32),
            vmem((M, C), F32),
            vmem((M, C), F32),
            vmem((M, C), F32),
            vmem((M, C), BF16),
            vmem((Q, M, H), F32),
            vmem((Q, M, H), F32),
            vmem((2, Q, M, H), F32),
            vmem((Q, 2, Q, M, H), F32),
            vmem((2, Q * M, H), F32),
            vmem((RPQ, rows * pad, H), BF16),
            vmem((R, rows * pad, H), BF16),
            vmem((R * rows * pad, H), F32),
            vmem((3, Q, R, piece, H), BF16),
            vmem((3, Q, R, piece, H), BF16),
            vmem((3, R, piece, H), F32),
            vmem((3, NP, piece, H), BF16),
            vmem((3, NP, piece, H), BF16),
            vmem((3, NP, piece, H), BF16),
            dma((9,)),
            dma((4, R)), dma((2, R)),
            dma((2, Q, Q)), dma((Q, 2, Q)),
            dma((Q,)), dma((Q,)),
            dma((R,)), dma((R,)),
            pltpu.SemaphoreType.REGULAR, dma((Q,)), dma,
            dma((3, Q)), dma((3, Q)),
            dma((3,)), dma((3,)),
            dma((3,)), dma((3,)),
            dma((3, Q)), dma((3, Q)),
        ],
        compiler_params=pltpu.CompilerParams(
            collective_id=0, has_side_effects=True, vmem_limit_bytes=60 * 1024 * 1024
        ),
        name="triangle_step",
    )(
        pair_rep.reshape(M, C), cotangent.reshape(M, C), ng.reshape(1, C), nb.reshape(1, C),
        pw, gw, tg.reshape(1, H), tb.reshape(1, H), ow,
    )
    outs = pl.pallas_call(
        functools.partial(finish, Q, R, piece, C, H),
        out_shape=(
            shapes[0],
            shapes[1],
            jax.ShapeDtypeStruct((C, 4 * H), F32),
            jax.ShapeDtypeStruct((C, C), F32),
            jax.ShapeDtypeStruct((H, C), F32),
        ),
        in_specs=[spec] * 3,
        out_specs=[spec] * 5,
        compiler_params=pltpu.CompilerParams(vmem_limit_bytes=4 * 1024 * 1024),
        name="finish",
    )(*parts)
    return (
        outs[0].reshape(rows, K, C), outs[1].reshape(rows, K, C), outs[2], outs[3], outs[4],
    )


def solution(mesh):
    tile = P(("crop", "row"), "col", None)
    grad = P("crop", None)
    return jax.shard_map(
        functools.partial(local, mesh.shape["row"], mesh.shape["col"]),
        mesh=mesh,
        in_specs=(tile, tile, P(), P(), P(), P(), P(), P(), P()),
        out_specs=(tile, tile, grad, grad, grad),
        check_vma=False,
    )
```

```python
import functools

import jax
import jax.numpy as jnp
from jax import lax
from jax.experimental import pallas as pl
from jax.experimental.pallas import tpu as pltpu
from jax.sharding import PartitionSpec as P

F32 = jnp.float32
BF16 = jnp.bfloat16


def mean_last(values):
    return jnp.mean(values, axis=-1, keepdims=True)


def normalise(values):
    centred = values - mean_last(values)
    inverse = lax.rsqrt(mean_last(centred * centred) + 1e-05)
    return centred * inverse, inverse


def norm_back(weighted, scaled, inverse):
    return inverse * (weighted - mean_last(weighted) - scaled * mean_last(weighted * scaled))


def dot(a, b, ca=1, cb=0):
    return lax.dot_general(a, b, (((ca,), (cb,)), ((), ())), preferred_element_type=F32)


def kernel(
    R, Q, rows, K, H, C,
    x_hbm, cot_hbm, ng_hbm, nb_hbm, pw_hbm, gw_hbm, tg_hbm, tb_hbm, ow_hbm,
    out_ref, pg_ref, gall_ref,
    x_ref, cot_ref, ng_ref, nb_ref, pw_ref, gw_ref, tg_ref, tb_ref, ow_ref,
    gath, right32, left32, coef, og_s, hat_s, inv_s, dupd_s, dn,
    hat2_s, tri_s, tri_rcv, d32, dsend, drecv, dcol32,
    csend, crecv, gkeep, gsend, grecv, gfin,
    in_s, gath_ss, gath_rs, tri_ss, tri_rs, dn_ss, dn_rs, dcol_ss, dcol_rs,
    near, hand_ss, hand_rs, cs_ss, cs_rs, gs_ss, gs_rs, gf_ss, gf_rs, sh_ss, sh_rs,
):
    r = lax.axis_index("row")
    q = lax.axis_index("col")
    M = rows * K
    N = rows * R
    NP = R * Q
    RPQ = R // Q
    pad = -(-rows // 8) * 8
    me = q * R + r
    direct_in, direct_out = (False, False, False), (False, True, True)
    mine_pieces = pl.ds(q * R, R)

    def remote(src, dst, ss, rs, rr, qq):
        return pltpu.make_async_remote_copy(
            src_ref=src, dst_ref=dst, send_sem=ss, recv_sem=rs,
            device_id={"row": rr, "col": qq}, device_id_type=pl.DeviceIdType.MESH,
        )

    def loop(lo, hi, body):
        if hi - lo <= 16:
            for t in range(lo, hi):
                body(t)
            return

        def step(t, carry):
            body(t)
            return carry
        lax.fori_loop(lo, hi, step, 0)

    def wrap(value, size):
        return jnp.where(value >= size, value - size, value)

    def peer(t):
        rr, qq = wrap(r + t // Q, R), wrap(q + t % Q, Q)
        return rr, qq, rr * Q + qq

    B = 2 if R > 1 and not R & (R - 1) else 1

    def mate(t):
        if R & (R - 1):
            return lax.rem(r + t, R)
        out, bit = 0, 1
        while bit < R:
            out = out + bit * ((r // bit + t // bit) % 2)
            bit *= 2
        return out

    def back(t):
        return lax.rem(r + R - t, R) if R & (R - 1) else mate(t)

    barrier = pltpu.get_barrier_semaphore()

    A = R // B

    def signal(sem, rr, qq):
        pl.semaphore_signal(
            sem, inc=1, device_id={"row": rr, "col": qq}, device_id_type=pl.DeviceIdType.MESH
        )

    loop(1, A, lambda t: signal(barrier, mate(t * B), q))
    for t in range(1, B):
        signal(barrier, mate(t), q)
    for t in range(1, Q):
        signal(barrier, r, wrap(q + t, Q))

    fetch = [
        pltpu.make_async_copy(src, dst, in_s.at[n]) for n, (src, dst) in enumerate((
            (x_hbm, x_ref), (ng_hbm, ng_ref), (nb_hbm, nb_ref), (pw_hbm, pw_ref),
            (gw_hbm, gw_ref), (cot_hbm, cot_ref), (ow_hbm, ow_ref), (tg_hbm, tg_ref),
            (tb_hbm, tb_ref),
        ))
    ]
    for copy in fetch:
        copy.start()

    piece = 2 * C // NP
    per = NP // 2

    def core_copy(g, t, slot, other):
        return remote(
            csend.at[g, t], crecv.at[g, slot], cs_ss.at[g, t], cs_rs.at[g, slot], r, other
        )

    def core_start(g, first, second):
        both = (first, second)

        def part(qq, rr):
            whole = rr * Q + qq
            p = whole % per
            return both[whole // per][p * piece : (p + 1) * piece, :]
        if direct_in[g]:
            for rr in range(R):
                for qq in range(Q):
                    gsend[g, qq * R + rr] = part(qq, rr).astype(BF16)
            scatter_go(g)
            return
        for t in range(Q):
            other = wrap(q + t, Q)
            for rr in range(R):
                block = part(Q - 1, rr)
                for qq in range(Q - 1):
                    block = jnp.where(other == qq, part(qq, rr), block)
                if t:
                    csend[g, t, rr] = block.astype(BF16)
                else:
                    gkeep[g, rr] = block
            if t:
                core_copy(g, t, q, other).start()

    def targets(straight):
        return [(t, u) for t in range(R) for u in range(Q if straight else 1) if t or u]

    def scatter(g, t, u):
        rr, qq = (mate(t) if t else r), wrap(q + u, Q)
        return remote(
            gsend.at[g, qq * R + rr], grecv.at[g, me],
            gs_ss.at[g], gs_rs.at[g], rr, qq
        )

    def scatter_all(g):
        block = pl.ds(0, len(targets(direct_in[g])))
        return remote(
            gsend.at[g, block], grecv.at[g, block], gs_ss.at[g], gs_rs.at[g], r, q
        )

    def scatter_go(g):
        for t, u in targets(direct_in[g])[::-1]:
            scatter(g, t, u).start()
        grecv[g, me] = gsend[g, me]

    def scatter_start(g):
        if direct_in[g]:
            return
        total = gkeep[g]
        for t in range(1, Q):
            other = wrap(q + t, Q)
            core_copy(g, t, other, other).wait_recv()
            total = total + crecv[g, other].astype(F32)
        gsend[g, mine_pieces] = total.astype(BF16)
        scatter_go(g)

    def spread(g, t, u):
        rr, qq = (mate(t) if t else r), wrap(q + u, Q)
        return remote(gfin.at[g, me], gfin.at[g, me], gf_ss.at[g], gf_rs.at[g], rr, qq)

    def spread_all(g):
        block = pl.ds(0, len(targets(direct_out[g])))
        return remote(gfin.at[g, block], gfin.at[g, block], gf_ss.at[g], gf_rs.at[g], r, q)

    def spread_start(g):
        scatter_all(g).wait_recv()
        if direct_in[g]:
            parts = [grecv[g, p] for p in range(NP)]
        else:
            kept = grecv[g, mine_pieces]
            parts = [kept[p] for p in range(R)]
        total = parts[0].astype(F32)
        for p in parts[1:]:
            total = total + p.astype(F32)
        gfin[g, me] = (total / N).astype(BF16)
        for t, u in targets(direct_out[g]):
            spread(g, t, u).start()

    def share(g, t, other, slot):
        block = pl.ds(slot * R, R)
        return remote(
            gfin.at[g, block], gfin.at[g, block], sh_ss.at[g, t], sh_rs.at[g, slot], r, other
        )

    lead = 5 * M // 9 // 16 * 16 if B > 1 else 0
    far = range(max(B, R // 2), R, B) if lead else ()
    head, rest, whole = pl.ds(0, lead), pl.ds(lead, M - lead), pl.ds(0, M)

    def block_copy(kind, src, t, lane, other):
        span = (head, rest, whole, head)[kind]
        return remote(
            gath.at[src, span], gath.at[src, span], gath_ss.at[kind, t], gath_rs.at[lane, src],
            other, q,
        )

    def line_head(t):
        return block_copy(0, r, t, 0, mate(t))

    def gather(t):
        return block_copy(1 if parted(t) else 2, r, t, 1, mate(t))

    def parted(t):
        return bool(far) and t >= far[0]

    def relay(t):
        return block_copy(3, back(t), t, 0, mate(1))

    def head_wait(t):
        block_copy(0, back(t), t, 0, back(t)).wait_recv()

    def edge(gate, value):
        sig = jax.nn.sigmoid(gate)
        return (sig * value).astype(BF16).astype(F32), sig

    for n in range(3):
        fetch[n].wait()
    hat, inv = normalise(x_ref[...].astype(F32))
    normed = (hat * ng_ref[...] + nb_ref[...]).astype(BF16)
    hat_s[...] = hat
    inv_s[...] = jnp.broadcast_to(inv, hat.shape)
    gath[r] = normed

    for n in range(4, 9):
        fetch[n].wait()
    og = jax.nn.sigmoid(dot(normed, gw_ref[...]))
    og_s[...] = og
    d_update = (cot_ref[...].astype(F32) * og).astype(BF16)
    dupd_s[...] = d_update
    dn_own = dot(d_update, ow_ref[...], 1, 1) * tg_ref[...]
    dn_own = dn_own - mean_last(dn_own)
    dn[q] = dn_own
    for b in range(RPQ):
        parts = []
        for i in range(rows):
            block = dn_own[i * K + b * rows : i * K + (b + 1) * rows, :]
            if pad > rows:
                block = jnp.concatenate([block, jnp.zeros((pad - rows, H), F32)], axis=0)
            parts.append(block)
        dsend[b] = jnp.concatenate(parts, axis=0).astype(BF16)
    mine = r // RPQ == q

    @pl.when(mine)
    def _():
        drecv[r] = dsend[lax.rem(r, RPQ)]

    pl.semaphore_wait(barrier, A + B + Q - 3)
    for t in range(1, B):
        signal(near, mate(t), q)
    if B > 1:
        for t in far:
            line_head(t).start()
        gather(1).start()
        pl.semaphore_wait(near, B - 1)
        for t in range(B, R):
            gather(t).start()
    else:
        loop(1, R, lambda t: gather(t).start())

    def dn_copy(t, slot, other):
        return remote(dn.at[q], dn.at[slot], dn_ss.at[t], dn_rs.at[slot], r, other)

    for t in range(1, Q):
        dn_copy(t, q, wrap(q + t, Q)).start()

    def each_target(act):
        def one(b):
            target = q * RPQ + b

            @pl.when(target != r)
            def _():
                act(b, target)
        loop(0, RPQ, one)

    def col_copy(b, target):
        return remote(dsend.at[b], drecv.at[r], dcol_ss.at[b], dcol_rs.at[r], target, q)

    each_target(lambda b, target: col_copy(b, target).start())

    def hand_on(t, other):
        return remote(drecv, drecv, hand_ss.at[t], hand_rs, r, other)

    own = pl.multiple_of(r * M, 8)
    fetch[3].wait()
    proj = dot(normed, pw_ref[...])
    vl, vr = proj[:, H : 2 * H], proj[:, 3 * H :]
    left_edge, sl = edge(proj[:, :H], vl)
    right_edge, sr = edge(proj[:, 2 * H : 3 * H], vr)
    left32[pl.ds(own, M), :] = left_edge
    right32[pl.ds(own, M), :] = right_edge
    coef[0] = vl * sl * (1.0 - sl)
    coef[1] = sl
    coef[2] = vr * sr * (1.0 - sr)
    coef[3] = sr
    def arrive(t, odd):
        source = back(t)
        block_copy(1 if parted(t) else 2, source, t, 1, source).wait_recv()
        if parted(t) and odd:
            block_copy(0, source, t, 0, mate(1)).wait_recv()
        proj = dot(gath[source], pw_ref[...])
        place = pl.ds(pl.multiple_of(source * M, 8), M)
        left32[place, :] = edge(proj[:, :H], proj[:, H : 2 * H])[0]
        right32[place, :] = edge(proj[:, 2 * H : 3 * H], proj[:, 3 * H :])[0]
    def zeros():
        return tuple(jnp.zeros((K, H), F32) for _ in range(rows))

    def partial(part, half):
        ours, theirs = (left32, right32) if part == 0 else (right32, left32)
        base = half * (K * K)

        def step(k, accs):
            block = theirs[pl.ds(base + k, K, stride=K), :]
            return tuple(
                accs[i] + ours[pl.ds(own + i * K + k, 1), :] * block for i in range(rows)
            )
        accs = lax.fori_loop(0, K, step, zeros(), unroll=8)
        for i in range(rows):
            tri_s[part, half, i * K : (i + 1) * K, :] = accs[i]

    def tri_copy(part, half, t, slot, other):
        return remote(
            tri_s.at[part, half], tri_rcv.at[slot, part, half],
            tri_ss.at[part, half, t], tri_rs.at[slot, part, half], r, other,
        )

    split = B > 1 and RPQ % B == 0

    def pass_on(t):
        if parted(t * B):
            head_wait(t * B)
            relay(t * B).start()

    halves = [mate(g * RPQ) // RPQ if split else g for g in range(Q)]
    if not split:
        if B > 1:
            [pass_on(t) for t in range(1, A)]
            arrive(1, False)
            for t in range(2, R):
                arrive(t, t % 2 == 1)
        else:
            loop(1, R, lambda t: arrive(t, False))
    for g, half in enumerate(halves):
        if split:
            start = g * (RPQ // B) if B > 1 and RPQ % B == 0 else 0
            if g == 0:
                if B > 1:
                    first = min(3, A)
                    [pass_on(t) for t in range(1, first)]
                    arrive(1, False)
                    [pass_on(t) for t in range(first, A)]
            for u in range(start, start + RPQ // B):
                for v in range(B):
                    if u:
                        arrive(u * B + v, v == 1)
        for part in range(2):
            partial(part, half)
            for t in range(1, Q):
                tri_copy(part, half, t, q, wrap(q + t, Q)).start()

    @pl.when(mine)
    def _():
        def col_wait(t):
            source = back(t)
            remote(
                dsend.at[0], drecv.at[source], dcol_ss.at[0], dcol_rs.at[source], source, q
            ).wait_recv()
        loop(1, R, col_wait)
        for t in range(1, Q):
            hand_on(t, wrap(q + t, Q)).start()

    for t in range(1, Q):
        other = wrap(q + t, Q)
        dn_copy(t, other, other).wait_recv()

    def complete(part, which):
        sums, weights = [], []
        for half in which:
            for t in range(1, Q):
                other = wrap(q + t, Q)
                tri_copy(part, half, t, other, other).wait_recv()
        for half in which:
            triangle = tri_s[part, half]
            for t in range(1, Q):
                triangle = triangle + tri_rcv[wrap(q + t, Q), part, half]
            sums.append(triangle)
            if part == 0:
                weights.append(dn[half])
            else:
                weights += [
                    dcol32[pl.ds(half * (K * pad) + j, K, stride=pad), :] for j in range(rows)
                ]
        weighted = jnp.concatenate(weights, axis=0)
        tri_hat, tri_inv = normalise(jnp.concatenate(sums, axis=0))
        d_tri = tri_inv * (weighted - tri_hat * mean_last(weighted * tri_hat))
        d_tri = d_tri.astype(BF16).astype(F32)
        for n, half in enumerate(which):
            d32[part, pl.ds(pl.multiple_of(half * M, 8), M), :] = d_tri[n * M : (n + 1) * M, :]
            if part == 0:
                hat2_s[half] = tri_hat[n * M : (n + 1) * M, :]

    def pull(part, which, accs):
        theirs = right32 if part == 0 else left32
        for half in which:
            def step(j, accs, half=half):
                block = theirs[pl.ds(pl.multiple_of((half * K + j) * K, 8), K), :]
                return tuple(
                    accs[i] + d32[part, pl.ds(half * M + i * K + j, 1), :] * block
                    for i in range(rows)
                )
            accs = lax.fori_loop(0, K, step, accs, unroll=8)
        return accs

    normed = gath[r]

    def settle(part, accs):
        grad = jnp.concatenate(accs, axis=0)
        first = (grad * coef[2 * part]).astype(BF16)
        second = (grad * coef[2 * part + 1]).astype(BF16)
        wide = dot(normed, jnp.concatenate([first, second], axis=-1), 0, 0)
        core_start(1 + part, wide[:, :H], wide[:, H:])
        return [first, second]

    def strips():
        @pl.when(jnp.logical_not(mine))
        def _():
            hand_on(0, r // RPQ).wait_recv()

        def widen_col(t):
            dcol32[pl.ds(pl.multiple_of(t * rows * pad, 8), rows * pad), :] = drecv[t].astype(F32)
        loop(0, R, widen_col)

    def gates():
        tri_norm = (hat2_s[q] * tg_ref[...] + tb_ref[...]).astype(BF16)
        update = dot(tri_norm, ow_ref[...])
        og = og_s[...]
        out_ref[...] = (og * update).astype(BF16)
        d_gate = (cot_ref[...].astype(F32) * update * og * (1.0 - og)).astype(BF16)
        core_start(0, dot(normed, d_gate, 0, 0), dot(tri_norm, dupd_s[...], 0, 0))
        return d_gate

    soon, late = halves[: Q - 1], halves[Q - 1 :]
    complete(0, soon)
    accs = pull(0, soon, zeros())
    complete(0, late)
    d_gate = gates()
    d_proj = settle(0, pull(0, late, accs))
    scatter_start(0)
    strips()
    complete(1, soon)
    accs = pull(1, soon, zeros())
    scatter_start(1)
    complete(1, late)
    d_proj += settle(1, pull(1, late, accs))
    scatter_start(2)
    d_cat = jnp.concatenate(d_proj, axis=-1)
    d_normed = dot(d_cat, pw_ref[...], 1, 1) + dot(d_gate, gw_ref[...], 1, 1)
    pg_ref[...] = norm_back(d_normed * ng_ref[...], hat_s[...], inv_s[...])
    for g in range(3):
        spread_start(g)

    if B > 1:
        gather(1).wait_send()
        for t in range(B, R):
            gather(t).wait_send()
        for t in far:
            line_head(t).wait_send()
            relay(t).wait_send()
    else:
        loop(1, R, lambda t: gather(t).wait_send())
    for t in range(1, Q):
        other = wrap(q + t, Q)
        dn_copy(t, q, other).wait_send()
        for part in range(2):
            for half in range(Q):
                tri_copy(part, half, t, q, other).wait_send()
    each_target(lambda b, target: col_copy(b, target).wait_send())

    @pl.when(mine)
    def _():
        for t in range(1, Q):
            hand_on(t, wrap(q + t, Q)).wait_send()

    for g in range(3):
        spread_all(g).wait_recv()
        if not direct_out[g]:
            for t in range(1, Q):
                share(g, t, wrap(q + t, Q), q).start()
    for g in range(3):
        scatter_all(g).wait_send()
        spread_all(g).wait_send()
        if not direct_in[g]:
            for t in range(1, Q):
                core_copy(g, t, q, wrap(q + t, Q)).wait_send()
    for g in range(3):
        if not direct_out[g]:
            for t in range(1, Q):
                other = wrap(q + t, Q)
                share(g, t, other, other).wait_recv()
    gall_ref[...] = gfin[...]
    for g in range(3):
        if not direct_out[g]:
            for t in range(1, Q):
                share(g, t, wrap(q + t, Q), q).wait_send()


def finish(Q, R, piece, C, H, block_ref, grad_ref, gall_ref, out_ref, pg_ref, gp_ref, gg_ref, go_ref):
    out_ref[...] = block_ref[...]
    pg_ref[...] = grad_ref[...]
    targets = (
        (gg_ref, 0), (go_ref, 0), (gp_ref, 0), (gp_ref, H), (gp_ref, 2 * H), (gp_ref, 3 * H),
    )
    per = C // piece
    for t, (ref, col) in enumerate(targets):
        for p in range(per):
            whole = (t % 2) * per + p
            ref[p * piece : (p + 1) * piece, col : col + H] = gall_ref[t // 2, whole % Q * R + whole // Q].astype(F32)


def local(R, Q, pair_rep, cotangent, ng, nb, pw, gw, tg, tb, ow):
    rows, K, C = pair_rep.shape
    H = tg.shape[0]
    M = rows * K
    NP = R * Q
    RPQ = R // Q
    pad = -(-rows // 8) * 8
    piece = 2 * C // NP
    dma = pltpu.SemaphoreType.DMA
    vmem = pltpu.VMEM
    spec = pl.BlockSpec(memory_space=pltpu.VMEM)
    shapes = (
        jax.ShapeDtypeStruct((M, C), BF16),
        jax.ShapeDtypeStruct((M, C), F32),
        jax.ShapeDtypeStruct((3, NP, piece, H), BF16),
    )
    any_spec = pl.BlockSpec(memory_space=pl.ANY)
    parts = pl.pallas_call(
        functools.partial(kernel, R, Q, rows, K, H, C),
        out_shape=tuple(pltpu.VMEM(v.shape, v.dtype) for v in shapes),
        in_specs=[any_spec] * 9,
        out_specs=[spec] * 3,
        scratch_shapes=[
            vmem((M, C), BF16), vmem((M, C), BF16), vmem((1, C), F32), vmem((1, C), F32),
            vmem((C, 4 * H), BF16), vmem((C, C), BF16), vmem((1, H), F32), vmem((1, H), F32),
            vmem((H, C), BF16),
            vmem((R, M, C), BF16),
            vmem((R * M, H), F32),
            vmem((R * M, H), F32),
            vmem((4, M, H), F32),
            vmem((M, C), F32),
            vmem((M, C), F32),
            vmem((M, C), F32),
            vmem((M, C), BF16),
            vmem((Q, M, H), F32),
            vmem((Q, M, H), F32),
            vmem((2, Q, M, H), F32),
            vmem((Q, 2, Q, M, H), F32),
            vmem((2, Q * M, H), F32),
            vmem((RPQ, rows * pad, H), BF16),
            vmem((R, rows * pad, H), BF16),
            vmem((R * rows * pad, H), F32),
            vmem((3, Q, R, piece, H), BF16),
            vmem((3, Q, R, piece, H), BF16),
            vmem((3, R, piece, H), F32),
            vmem((3, NP, piece, H), BF16),
            vmem((3, NP, piece, H), BF16),
            vmem((3, NP, piece, H), BF16),
            dma((9,)),
            dma((4, R)), dma((2, R)),
            dma((2, Q, Q)), dma((Q, 2, Q)),
            dma((Q,)), dma((Q,)),
            dma((R,)), dma((R,)),
            pltpu.SemaphoreType.REGULAR, dma((Q,)), dma,
            dma((3, Q)), dma((3, Q)),
            dma((3,)), dma((3,)),
            dma((3,)), dma((3,)),
            dma((3, Q)), dma((3, Q)),
        ],
        compiler_params=pltpu.CompilerParams(
            collective_id=0, has_side_effects=True, vmem_limit_bytes=60 * 1024 * 1024
        ),
        name="triangle_step",
    )(
        pair_rep.reshape(M, C), cotangent.reshape(M, C), ng.reshape(1, C), nb.reshape(1, C),
        pw, gw, tg.reshape(1, H), tb.reshape(1, H), ow,
    )
    outs = pl.pallas_call(
        functools.partial(finish, Q, R, piece, C, H),
        out_shape=(
            shapes[0],
            shapes[1],
            jax.ShapeDtypeStruct((C, 4 * H), F32),
            jax.ShapeDtypeStruct((C, C), F32),
            jax.ShapeDtypeStruct((H, C), F32),
        ),
        in_specs=[spec] * 3,
        out_specs=[spec] * 5,
        compiler_params=pltpu.CompilerParams(vmem_limit_bytes=4 * 1024 * 1024),
        name="finish",
    )(*parts)
    return (
        outs[0].reshape(rows, K, C), outs[1].reshape(rows, K, C), outs[2], outs[3], outs[4],
    )


def solution(mesh):
    tile = P(("crop", "row"), "col", None)
    grad = P("crop", None)
    return jax.shard_map(
        functools.partial(local, mesh.shape["row"], mesh.shape["col"]),
        mesh=mesh,
        in_specs=(tile, tile, P(), P(), P(), P(), P(), P(), P()),
        out_specs=(tile, tile, grad, grad, grad),
        check_vma=False,
    )
```
